512 devices in a mesh: dp: 4 (over x), expert: 128 (over z, y, core).
Axes of the slice: x: 4, y: 8, z: 8, core: 2. Of those that a mesh axis runs over, the one named last changes fastest.
Arguments:
- tokens: bfloat16 [65536, 1024], P(('dp', 'expert')), may hold values from -6 to 6
- grad_out: bfloat16 [65536, 1024], P(('dp', 'expert')), may hold values from -0.75 to 0.75
- expert_ids: int32 [65536, 4], P(('dp', 'expert')), may hold values from 0 to 127, all different within a row; in each aligned block of 128 rows (0 to 127, 128 to 255, ...) at most 6 rows name the same one
- gate_weight: bfloat16 [65536, 4], P(('dp', 'expert')), may hold values from 0.049804688 to 1
- w_gate: bfloat16 [128, 1024, 384], P('expert'), may hold values from -0.1875 to 0.1875
- w_up: bfloat16 [128, 1024, 384], P('expert'), may hold values from -0.1875 to 0.1875
- w_down: bfloat16 [128, 384, 1024], P('expert'), may hold values from -0.3125 to 0.3125
Outputs:
- grad_tokens: bfloat16 [65536, 1024], P(('dp', 'expert'))
- grad_gate: bfloat16 [65536, 4], P(('dp', 'expert'))
- grad_w_gate: float32 [128, 1024, 384], P('expert', 'dp')
- grad_w_up: float32 [128, 1024, 384], P('expert', 'dp')
- grad_w_down: float32 [128, 384, 1024], P('expert', None, 'dp')
The draws below stay inside these ranges and needn't reach their ends.
Inputs may be any that keep to these rules, and one draw needn't show every extreme that they name: `expert_ids`: each row names 4 different experts; in the rows of one device no expert is named by more than 6 rows.
All inputs are finite; a program needn't handle non-finite values.
Results may differ from the reference program's by a relative error of at most 0.0085.
Values may be sent and summed in bfloat16 or wider, within the bound.
A program may use at most 64 MiB of HBM per device.

```python
import math
import jax
import jax.numpy as jnp
import numpy as np
from jax import lax

D = 1024
FF = 384
TOPK = 4
TOK_DEV = 128
EXPERTS = 128
MOST = 6
TOKENS = 65536
N_DP = 4
N_EXPERT = 128


def levels(stream_key, shape, pieces, least, top_value):
    def one(dim, blocks):
        draws = jax.random.uniform(jax.random.fold_in(jax.random.fold_in(stream_key, 6), dim), (blocks,), jnp.float32, least / len(pieces), top_value / len(pieces))
        return jnp.repeat(jnp.exp(draws), shape[dim] // blocks).reshape((-1,) + (1,) * (len(shape) - dim - 1))

    factor_of = one(*pieces[0])
    for cut in pieces[1:]:
        factor_of = factor_of * one(*cut)
    return factor_of


def assign_block(rng, own, number, rows, number_of, top, limit, skew):
    order = jax.random.permutation(rng, number_of)
    crowded, common = load_shares(number_of, rows * top, limit, skew, True), load_shares(number_of, rows * top, limit, skew, False)
    places = jnp.arange(number_of)

    def named(sizes, offset_by):
        used = int((sizes > 0).sum())
        fixed = max(1, used // 4)
        shifted = fixed + (places - fixed + offset_by * (used - fixed)) % max(1, number_of - fixed)
        return jnp.zeros((number_of,), jnp.int32).at[order[jnp.where(places < fixed, places, shifted)]].set(jnp.asarray(sizes, jnp.int32))

    sizes = jnp.where(number % 4 == 0, named(crowded, number // 4), named(common, number - number // 4 - 1))
    mixed = jax.random.permutation(jax.random.fold_in(own, 3), number_of)
    source_of, sink = mixed[0:number_of // 2 * 2:2], mixed[1:number_of // 2 * 2:2]
    slack = jnp.minimum(sizes[source_of] - 1, limit - sizes[sink]) // 2
    slack = jnp.where((source_of == order[0]) | (sink == order[0]) | (sizes[sink] == 0), 0, jnp.maximum(slack, 0))
    shifted = jax.random.randint(jax.random.fold_in(own, 4), (number_of // 2,), 0, 1 << 20) % (slack + 1)
    sizes = sizes.at[source_of].add(-shifted).at[sink].add(shifted)
    items = jnp.searchsorted(jnp.cumsum(sizes), jnp.arange(rows * top), side="right").astype(jnp.int32)
    table = items.reshape(top, rows).T
    table = table[jax.random.permutation(jax.random.fold_in(own, 1), rows)]
    offset_by = jax.random.randint(jax.random.fold_in(own, 2), (rows, 1), 0, top)
    return jnp.take_along_axis(table, (jnp.arange(top)[None, :] + offset_by) % top, axis=1)


def load_shares(number_of, total, most, slope, full):
    weights = [(1 << 20) // math.isqrt(standing ** slope) + 1 for standing in range(1, number_of + 1)]
    largest = most if full else min(most, max(-(-total // number_of), total * weights[0] // sum(weights)))
    least = 1 if total - largest >= number_of - 1 else 0
    counts, surplus = [largest] + [least] * (number_of - 1), total - largest - least * (number_of - 1)
    while surplus > 0:
        movable = [i for i in range(1, number_of) if counts[i] < largest] or [i for i in range(1, number_of) if counts[i] < most]
        mass, remaining = sum([weights[i] for i in movable]), surplus
        for i in movable:
            extra = min(most - counts[i], max(1, remaining * weights[i] // mass), surplus)
            counts[i] = counts[i] + extra
            surplus = surplus - extra
    return np.array(counts)


def bell_draw(own_key, shape, spread, most, split=(), held_as=jnp.bfloat16):
    array = jax.random.normal(own_key, shape, jnp.float32) * spread
    if len(split) > 0:
        array = levels(own_key, shape, split, -0.22, 0.18) * array
    return jnp.clip(array, min=-most, max=most).astype(held_as)


def setup_inputs(seed: int = 0) -> dict:
    keys = jax.random.split(jax.random.key(seed), 8)
    tokens = bell_draw(keys[0], (TOKENS, D), 1.0, 6.0, ((0, 512),))
    grad_out = bell_draw(keys[1], (TOKENS, D), 0.125, 0.75, ((0, 512),))
    expert_ids_keys = jax.random.split(jax.random.fold_in(keys[2], 1), TOKENS // TOK_DEV)
    expert_ids_turns = jax.random.permutation(jax.random.fold_in(keys[2], 3), TOKENS // TOK_DEV)
    expert_ids = jax.vmap(lambda own, number: assign_block(jax.random.fold_in(keys[2], 2), own, number, TOK_DEV, EXPERTS, TOPK, MOST, 2))(expert_ids_keys, expert_ids_turns).reshape((TOKENS, TOPK))
    gate_weight = jnp.clip(jnp.exp(math.log(1.0) - 2.9996462 * jax.random.uniform(keys[3], (TOKENS, TOPK), jnp.float32) ** levels(keys[3], (TOKENS, TOPK), ((0, 512),), -0.2, 0.2)), 0.049804688, 1.0).astype(jnp.bfloat16)
    w_gate = bell_draw(keys[4], (EXPERTS, D, FF), D ** -0.5, 0.1875, ((0, 128),))
    w_up = bell_draw(keys[5], (EXPERTS, D, FF), D ** -0.5, 0.1875, ((0, 128),))
    w_down = bell_draw(keys[6], (EXPERTS, FF, D), FF ** -0.5, 0.3125, ((0, 128),))
    return dict(tokens=tokens, grad_out=grad_out, expert_ids=expert_ids, gate_weight=gate_weight, w_gate=w_gate, w_up=w_up, w_down=w_down)


def forward_tile(inputs, weights):
    gate_matrix, up_matrix, down_matrix = weights
    pre_gate = jnp.dot(inputs, gate_matrix, preferred_element_type=jnp.float32)
    pre_up = jnp.dot(inputs, up_matrix, preferred_element_type=jnp.float32)
    hidden = (jax.nn.silu(pre_gate) * pre_up).astype(jnp.bfloat16)
    return pre_gate, pre_up, hidden


def backward_tile(inputs, pre_gate, pre_up, hidden, upstream, gate_rows, weights):
    gate_matrix, up_matrix, down_matrix = weights
    across = (((1,), (1,)), ((), ()))
    down_rows = (((0,), (0,)), ((), ()))
    outputs = jnp.dot(hidden, down_matrix, preferred_element_type=jnp.float32)
    upstream_wide = upstream.astype(jnp.float32)
    gate_grad = jnp.sum(outputs * upstream_wide, axis=1).astype(jnp.bfloat16)
    scaled = (gate_rows.astype(jnp.float32)[:, None] * upstream_wide).astype(jnp.bfloat16)
    hidden_grad = lax.dot_general(scaled, down_matrix, across, preferred_element_type=jnp.float32)
    logistic = jax.nn.sigmoid(pre_gate)
    d_gate = (hidden_grad * pre_up * logistic * (1.0 + pre_gate * (1.0 - logistic))).astype(jnp.bfloat16)
    d_up = (hidden_grad * jax.nn.silu(pre_gate)).astype(jnp.bfloat16)
    route_grad = (lax.dot_general(d_gate, gate_matrix, across, preferred_element_type=jnp.float32)
                  + lax.dot_general(d_up, up_matrix, across, preferred_element_type=jnp.float32)).astype(jnp.bfloat16)
    grad_terms = (lax.dot_general(inputs, d_gate, down_rows, preferred_element_type=jnp.float32),
                  lax.dot_general(inputs, d_up, down_rows, preferred_element_type=jnp.float32),
                  lax.dot_general(hidden, scaled, down_rows, preferred_element_type=jnp.float32))
    return route_grad, gate_grad, grad_terms


def reference(tokens, grad_out, expert_ids, gate_weight, w_gate, w_up, w_down):
    group = TOK_DEV * N_EXPERT
    route_count = group * TOPK
    capacity = N_EXPERT * MOST
    replica_tokens = tokens.reshape(N_DP, group, D)
    replica_upstream = grad_out.reshape(N_DP, group, D)
    replica_ids = expert_ids.reshape(N_DP, route_count)
    replica_gates = gate_weight.reshape(N_DP, route_count)

    def one_replica(expert, route_ids, gate_list, inputs_all, upstream_all, weights):
        chosen = route_ids == expert
        ranked = (jnp.cumsum(chosen.astype(jnp.int32)) - 1).astype(jnp.int32)
        target = jnp.where(chosen, ranked, capacity).astype(jnp.int32)
        source = jnp.full((capacity,), route_count, jnp.int32).at[target].set(
            jnp.arange(route_count, dtype=jnp.int32), mode="drop")
        owner_token = (source // TOPK).astype(jnp.int32)
        inputs = inputs_all.at[owner_token].get(mode="fill", fill_value=0)
        upstream = upstream_all.at[owner_token].get(mode="fill", fill_value=0)
        gate_rows = gate_list.at[source].get(mode="fill", fill_value=0)
        pre_gate, pre_up, hidden = forward_tile(inputs, weights)
        route_grad, gate_grad, grad_terms = backward_tile(inputs, pre_gate, pre_up, hidden, upstream, gate_rows, weights)
        return source, owner_token, route_grad, gate_grad, grad_terms

    def add_rows(total, index, values):
        return total.at[index].add(values, mode="drop")

    def set_rows(total, index, values):
        return total.at[index].set(values, mode="drop")

    def per_expert(carry, expert):
        token_total, gate_total = carry
        weights = (w_gate[expert], w_up[expert], w_down[expert])
        source, owner_token, route_grad, gate_grad, grad_terms = jax.vmap(
            one_replica, in_axes=(None, 0, 0, 0, 0, None))(
            expert, replica_ids, replica_gates, replica_tokens, replica_upstream, weights)
        token_total = jax.vmap(add_rows)(token_total, owner_token, route_grad.astype(jnp.float32))
        gate_total = jax.vmap(set_rows)(gate_total, source, gate_grad.astype(jnp.float32))
        grads = tuple(jnp.sum(lax.optimization_barrier(term.astype(jnp.bfloat16)).astype(jnp.float32), axis=0)
                      for term in grad_terms)
        return (token_total, gate_total), grads

    start = (jnp.zeros((N_DP, group, D), jnp.float32), jnp.zeros((N_DP, route_count), jnp.float32))
    (token_total, gate_total), grads = lax.scan(per_expert, start, jnp.arange(EXPERTS, dtype=jnp.int32))
    grad_tokens = token_total.reshape(TOKENS, D).astype(jnp.bfloat16)
    grad_gate = gate_total.reshape(TOKENS, TOPK).astype(jnp.bfloat16)
    return grad_tokens, grad_gate, grads[0], grads[1], grads[2]
```

```python
import functools

import jax
import jax.numpy as jnp
from jax import lax
from jax.experimental import pallas as pl
from jax.experimental.pallas import tpu as pltpu
from jax.sharding import PartitionSpec as P

F32, BF16 = jnp.float32, jnp.bfloat16
SLOTS = 6
BLOCK = 8
ROWS = 1024
CH = 256
VMEM = pl.BlockSpec(memory_space=pltpu.VMEM)


def dot(a, b, contract=((1,), (0,))):
    return lax.dot_general(a, b, (contract, ((), ())), preferred_element_type=F32)


def iota(shape, dim):
    return lax.broadcasted_iota(jnp.int32, shape, dim)


def one_hots(ids):
    experts = iota((128, 128), 0)
    named = jnp.zeros((128, 128), F32)
    for k in range(4):
        named = named + jnp.where(ids[k : k + 1, :] == experts, 1.0, 0.0)
    named = named.astype(BF16)
    earlier = jnp.where(iota((128, 128), 0) < iota((128, 128), 1), 1.0, 0.0).astype(BF16)
    rank = dot(named, earlier)
    rank = jnp.where(named.astype(F32) > 0.5, rank, -1.0).astype(BF16)
    spread = jnp.where(iota((ROWS, 128), 0) // BLOCK == iota((ROWS, 128), 1), 1.0, 0.0).astype(BF16)
    ranks = dot(spread, rank)
    place = (iota((ROWS, 128), 0) % BLOCK).astype(F32)
    main = jnp.where((ranks == place) & (place < 5.5), 1.0, 0.0)
    tails = [
        jnp.where((ranks == 3.0 * (place - 6.0) + j) & (place > 5.5), 1.0, 0.0) for j in range(3)
    ]
    return spread, main, tails


def pack_kernel(ids_ref, gate_ref, tok_ref, up_ref, out_ref):
    ids = ids_ref[...]
    spread, main, tails = one_hots(ids)
    gates = gate_ref[...].astype(F32)
    experts = iota((128, 128), 0)
    gate_of = jnp.zeros((128, 128), F32)
    for k in range(4):
        gate_of = gate_of + jnp.where(ids[k : k + 1, :] == experts, gates[k : k + 1, :], 0.0)
    gate_rows = dot(spread, gate_of.astype(BF16))
    for j in range(3):
        gate_col = jnp.sum((main + tails[j]) * gate_rows, axis=1, keepdims=True)
        pick = jnp.concatenate([main.astype(BF16), tails[j].astype(BF16)], axis=1)
        for which, ref in enumerate((tok_ref, up_ref)):
            both = jnp.concatenate(
                [ref[:, j * CH : (j + 1) * CH], ref[:, 3 * CH : 4 * CH]], axis=0
            )
            rows = dot(pick, both)
            if which == 1:
                rows = rows * gate_col
            base = which * 3 * CH + j * CH
            out_ref[:, :, base : base + CH] = rows.astype(BF16).reshape(128, BLOCK, CH)


def compute_kernel(
    got_ref, wg_ref, wu_ref, wd_ref, back_ref, gg_ref, gu_ref, gd_ref, x_s, s_s, dg_s, du_s, h_s
):
    row, col = iota((CH, CH), 0), iota((CH, CH), 1)
    same = row // BLOCK == col // BLOCK
    ra, ca = row % BLOCK, col % BLOCK
    unpack = jnp.concatenate(
        [
            jnp.where(same & (ra < 6) & (ca == 6 + ra // 3) & (ra % 3 == j), 1.0, 0.0)
            for j in range(3)
        ],
        axis=1,
    ).astype(BF16)
    repack = [
        jnp.where(same & (ra >= 6) & (ca == 3 * (ra - 6) + j), 1.0, 0.0).astype(BF16)
        for j in range(3)
    ]
    real = (iota((CH, 1), 0) % BLOCK) < SLOTS
    lane = iota((CH, 128), 1)

    def group(i, _):
        rows = pl.ds(pl.multiple_of(i * CH, CH), CH)
        srcs = pl.ds(pl.multiple_of(i * (CH // BLOCK), CH // BLOCK), CH // BLOCK)
        for which, ref in enumerate((x_s, s_s)):
            parts = []
            for j in range(3):
                base = which * 3 * CH + j * CH
                part = got_ref[srcs, :, base : base + CH].reshape(CH, CH)
                ref[rows, j * CH : (j + 1) * CH] = part
                parts.append(part)
            ref[rows, 3 * CH :] = dot(unpack, jnp.concatenate(parts, axis=0)).astype(BF16)
        x, s = x_s[rows, :], s_s[rows, :]
        pre_gate = dot(x, wg_ref[...])
        pre_up = dot(x, wu_ref[...])
        sig = jax.nn.sigmoid(pre_gate)
        silu = pre_gate * sig
        hidden = jnp.where(real, silu * pre_up, 0.0).astype(BF16)
        hgrad = dot(s, wd_ref[...], ((1,), (1,)))
        d_gate = jnp.where(
            real, hgrad * pre_up * sig * (1.0 + pre_gate * (1.0 - sig)), 0.0
        ).astype(BF16)
        d_up = jnp.where(real, hgrad * silu, 0.0).astype(BF16)
        h_s[rows, :] = hidden
        dg_s[rows, :] = d_gate
        du_s[rows, :] = d_up
        product = jnp.sum(hidden.astype(F32) * hgrad, axis=1, keepdims=True)
        back_ref[srcs, :, 3 * CH :] = (
            jnp.broadcast_to(product, (CH, 128)).astype(BF16).reshape(CH // BLOCK, BLOCK, 128)
        )
        tail = dot(d_gate, wg_ref[3 * CH :, :], ((1,), (1,))) + dot(
            d_up, wu_ref[3 * CH :, :], ((1,), (1,))
        )
        tail = tail.astype(BF16)
        for j in range(3):
            cols = slice(j * CH, (j + 1) * CH)
            part = dot(d_gate, wg_ref[cols, :], ((1,), (1,))) + dot(
                d_up, wu_ref[cols, :], ((1,), (1,))
            )
            part = part + dot(repack[j], tail)
            back_ref[srcs, :, cols] = part.astype(BF16).reshape(CH // BLOCK, BLOCK, CH)
        return 0

    lax.fori_loop(0, ROWS // CH, group, 0)

    def grads(i, _):
        cols = pl.ds(pl.multiple_of(i * CH, CH), CH)
        x = x_s[:, cols]
        gg_ref[cols, :] = dot(x, dg_s[...], ((0,), (0,))).astype(BF16)
        gu_ref[cols, :] = dot(x, du_s[...], ((0,), (0,))).astype(BF16)
        gd_ref[:, cols] = dot(h_s[...], s_s[:, cols], ((0,), (0,))).astype(BF16)
        return 0

    lax.fori_loop(0, 4, grads, 0)


def combine_kernel(ids_ref, gate_ref, back_ref, tok_ref, gate_out_ref):
    ids = ids_ref[...]
    spread, main, tails = one_hots(ids)
    main16 = main.astype(BF16)
    last = jnp.zeros((128, CH), F32)
    for j in range(3):
        part = back_ref[:, :, j * CH : (j + 1) * CH].reshape(ROWS, CH)
        tok_ref[:, j * CH : (j + 1) * CH] = dot(main16, part, ((0,), (0,))).astype(BF16)
        last = last + dot(tails[j].astype(BF16), part, ((0,), (0,)))
    tok_ref[:, 3 * CH :] = last.astype(BF16)
    product = back_ref[:, :, 3 * CH :].reshape(ROWS, 128)
    mine = dot(spread, (main * product.astype(F32)).astype(BF16), ((0,), (0,)))
    gates = gate_ref[...].astype(F32)
    experts = iota((128, 128), 0)
    for k in range(4):
        total = jnp.sum(jnp.where(ids[k : k + 1, :] == experts, mine, 0.0), axis=0, keepdims=True)
        gate_out_ref[k : k + 1, :] = (total / gates[k : k + 1, :]).astype(BF16)


def local(kernel, out_shape, args, scratch=(), name=None):
    return pl.pallas_call(
        kernel,
        out_shape=out_shape,
        in_specs=[VMEM] * len(args),
        out_specs=jax.tree.map(lambda _: VMEM, out_shape),
        scratch_shapes=scratch,
        compiler_params=pltpu.CompilerParams(vmem_limit_bytes=48 << 20),
        name=name,
    )(*args)


def shape(*dims, dtype=BF16):
    return jax.ShapeDtypeStruct(dims, dtype)


def shards(tokens, grad_out, expert_ids, gate_weight, w_gate, w_up, w_down):
    ids, gates = expert_ids.T, gate_weight.T
    send = local(pack_kernel, shape(128, BLOCK, 6 * CH), (ids, gates, tokens, grad_out), name="pack")
    got = lax.all_to_all(send, "expert", split_axis=0, concat_axis=0, tiled=True)
    back, part_gate, part_up, part_down = local(
        compute_kernel,
        (shape(128, BLOCK, 3 * CH + 128), shape(1024, 384), shape(1024, 384), shape(384, 1024)),
        (got, w_gate[0], w_up[0], w_down[0]),
        scratch=[
            pltpu.VMEM((ROWS, 1024), BF16),
            pltpu.VMEM((ROWS, 1024), BF16),
            pltpu.VMEM((ROWS, 384), BF16),
            pltpu.VMEM((ROWS, 384), BF16),
            pltpu.VMEM((ROWS, 384), BF16),
        ],
        name="compute",
    )
    home = lax.all_to_all(back, "expert", split_axis=0, concat_axis=0, tiled=True)
    grad_tokens, grad_gate = local(
        combine_kernel, (shape(128, 1024), shape(4, 128)), (ids, gates, home), name="combine"
    )
    sums = [
        lax.psum_scatter(part, "dp", scatter_dimension=dim, tiled=True).astype(F32)[None]
        for part, dim in ((part_gate, 0), (part_up, 0), (part_down, 1))
    ]
    return (grad_tokens, grad_gate.T, *sums)


def solution(mesh):
    rows = P(("dp", "expert"), None)
    weights = P("expert", None, None)
    return jax.shard_map(
        shards,
        mesh=mesh,
        in_specs=(rows, rows, rows, rows, weights, weights, weights),
        out_specs=(rows, rows, P("expert", "dp", None), P("expert", "dp", None), P("expert", None, "dp")),
        check_vma=False,
    )
```

```python
import functools

import jax
import jax.numpy as jnp
from jax import lax
from jax.experimental import pallas as pl
from jax.experimental.pallas import tpu as pltpu
from jax.sharding import PartitionSpec as P

F32, BF16 = jnp.float32, jnp.bfloat16
SLOTS = 6
BLOCK = 8
ROWS = 1024
CH = 256
VMEM = pl.BlockSpec(memory_space=pltpu.VMEM)


def dot(a, b, contract=((1,), (0,))):
    return lax.dot_general(a, b, (contract, ((), ())), preferred_element_type=F32)


def iota(shape, dim):
    return lax.broadcasted_iota(jnp.int32, shape, dim)


def one_hots(ids):
    experts = iota((128, 128), 0)
    named = jnp.zeros((128, 128), F32)
    for k in range(4):
        named = named + jnp.where(ids[k : k + 1, :] == experts, 1.0, 0.0)
    named = named.astype(BF16)
    earlier = jnp.where(iota((128, 128), 0) < iota((128, 128), 1), 1.0, 0.0).astype(BF16)
    rank = dot(named, earlier)
    rank = jnp.where(named.astype(F32) > 0.5, rank, -1.0)
    spread = jnp.where(iota((ROWS, 128), 0) // BLOCK == iota((ROWS, 128), 1), 1.0, 0.0).astype(BF16)
    ranks = dot(spread, rank.astype(BF16))
    place = (iota((ROWS, 128), 0) % BLOCK).astype(F32)
    main = jnp.where((ranks == place) & (place < 5.5), 1.0, 0.0)
    tails = [
        jnp.where((ranks == 3.0 * (place - 6.0) + j) & (place > 5.5), 1.0, 0.0) for j in range(3)
    ]
    return rank, main, tails, spread


def put_chunk(halves, blocks, j, rows):
    low, high = halves
    count = rows.shape[0] // BLOCK
    if j == 0:
        low[blocks, :, 0:256] = rows.reshape(count, BLOCK, CH)
    elif j == 1:
        low[blocks, :, 256:384] = rows[:, 0:128].reshape(count, BLOCK, 128)
        high[blocks, :, 0:128] = rows[:, 128:256].reshape(count, BLOCK, 128)
    else:
        high[blocks, :, 128:384] = rows.reshape(count, BLOCK, CH)


def get_chunk(halves, blocks, j):
    low, high = halves
    if j == 0:
        return low[blocks, :, 0:256].reshape(-1, CH)
    if j == 1:
        left = low[blocks, :, 256:384].reshape(-1, 128)
        return jnp.concatenate([left, high[blocks, :, 0:128].reshape(-1, 128)], axis=1)
    return high[blocks, :, 128:384].reshape(-1, CH)


def pack_kernel(ids_ref, gate_ref, tok_ref, up_ref, xa_ref, xb_ref, sa_ref, sb_ref):
    ids = ids_ref[...]
    _, main, tails, spread = one_hots(ids)
    gates = gate_ref[...].astype(F32)
    experts = iota((128, 128), 0)
    gate_of = jnp.zeros((128, 128), F32)
    for k in range(4):
        gate_of = gate_of + jnp.where(ids[k : k + 1, :] == experts, gates[k : k + 1, :], 0.0)
    gate_rows = dot(spread, gate_of.astype(BF16))
    for j in range(3):
        gate_col = jnp.sum((main + tails[j]) * gate_rows, axis=1, keepdims=True)
        pick = jnp.concatenate([main.astype(BF16), tails[j].astype(BF16)], axis=1)
        for which, ref in enumerate((tok_ref, up_ref)):
            both = jnp.concatenate(
                [ref[:, j * CH : (j + 1) * CH], ref[:, 3 * CH : 4 * CH]], axis=0
            )
            rows = dot(pick, both)
            if which == 1:
                rows = rows * gate_col
            halves = ((xa_ref, xb_ref), (sa_ref, sb_ref))[which]
            put_chunk(halves, slice(None), j, rows.astype(BF16))


def compute_kernel(
    xa_ref, xb_ref, sa_ref, sb_ref, wg_ref, wu_ref, wd_ref,
    ba_ref, bb_ref, p_ref, gg_ref, gu_ref, gd_ref, x_s, s_s, dg_s, du_s, h_s
):
    row, col = iota((CH, CH), 0), iota((CH, CH), 1)
    same = row // BLOCK == col // BLOCK
    ra, ca = row % BLOCK, col % BLOCK
    unpack = jnp.concatenate(
        [
            jnp.where(same & (ra < 6) & (ca == 6 + ra // 3) & (ra % 3 == j), 1.0, 0.0)
            for j in range(3)
        ],
        axis=1,
    ).astype(BF16)
    repack = [
        jnp.where(same & (ra >= 6) & (ca == 3 * (ra - 6) + j), 1.0, 0.0).astype(BF16)
        for j in range(3)
    ]
    real = (iota((CH, 1), 0) % BLOCK) < SLOTS
    lane = iota((CH, 128), 1)

    def group(i, _):
        rows = pl.ds(pl.multiple_of(i * CH, CH), CH)
        srcs = pl.ds(pl.multiple_of(i * (CH // BLOCK), CH // BLOCK), CH // BLOCK)
        for which, ref in enumerate((x_s, s_s)):
            parts = []
            for j in range(3):
                part = get_chunk(((xa_ref, xb_ref), (sa_ref, sb_ref))[which], srcs, j)
                ref[rows, j * CH : (j + 1) * CH] = part
                parts.append(part)
            ref[rows, 3 * CH :] = dot(unpack, jnp.concatenate(parts, axis=0)).astype(BF16)
        x, s = x_s[rows, :], s_s[rows, :]
        pre_gate = dot(x, wg_ref[...])
        pre_up = dot(x, wu_ref[...])
        sig = jax.nn.sigmoid(pre_gate)
        silu = pre_gate * sig
        hidden = jnp.where(real, silu * pre_up, 0.0).astype(BF16)
        hgrad = dot(s, wd_ref[...], ((1,), (1,)))
        d_gate = jnp.where(
            real, hgrad * pre_up * sig * (1.0 + pre_gate * (1.0 - sig)), 0.0
        ).astype(BF16)
        d_up = jnp.where(real, hgrad * silu, 0.0).astype(BF16)
        h_s[rows, :] = hidden
        dg_s[rows, :] = d_gate
        du_s[rows, :] = d_up
        product = jnp.sum(hidden.astype(F32) * hgrad, axis=1, keepdims=True)
        spots = jnp.where(lane == iota((CH, 128), 0) % BLOCK, product, 0.0)
        p_ref[srcs, 0, :] = jnp.sum(spots.reshape(CH // BLOCK, BLOCK, 128), axis=1)
        tail = dot(d_gate, wg_ref[3 * CH :, :], ((1,), (1,))) + dot(
            d_up, wu_ref[3 * CH :, :], ((1,), (1,))
        )
        tail = tail.astype(BF16)
        for j in range(3):
            cols = slice(j * CH, (j + 1) * CH)
            part = dot(d_gate, wg_ref[cols, :], ((1,), (1,))) + dot(
                d_up, wu_ref[cols, :], ((1,), (1,))
            )
            part = part + dot(repack[j], tail)
            put_chunk((ba_ref, bb_ref), srcs, j, part.astype(BF16))
        return 0

    lax.fori_loop(0, ROWS // CH, group, 0)

    def grads(i, _):
        cols = pl.ds(pl.multiple_of(i * CH, CH), CH)
        x = x_s[:, cols]
        gg_ref[i] = dot(x, dg_s[...], ((0,), (0,))).astype(BF16)
        gu_ref[i] = dot(x, du_s[...], ((0,), (0,))).astype(BF16)
        gd_ref[i] = dot(h_s[...], s_s[:, cols], ((0,), (0,))).astype(BF16)
        return 0

    lax.fori_loop(0, 4, grads, 0)


def combine_kernel(
    ids_ref, gate_ref, ba_ref, bb_ref, p_ref, rg_ref, ru_ref, rd_ref,
    tok_ref, gate_out_ref, gg_ref, gu_ref, gd_ref
):
    for part, total in ((rg_ref, gg_ref), (ru_ref, gu_ref), (rd_ref, gd_ref)):
        total[0] = sum(part[i].astype(F32) for i in range(1, 4)) + part[0].astype(F32)
    ids = ids_ref[...]
    rank, main, tails, _ = one_hots(ids)
    main = main.astype(BF16)
    last = jnp.zeros((128, CH), F32)
    for j in range(3):
        part = get_chunk((ba_ref, bb_ref), slice(None), j)
        tok_ref[:, j * CH : (j + 1) * CH] = dot(main, part, ((0,), (0,))).astype(BF16)
        last = last + dot(tails[j].astype(BF16), part, ((0,), (0,)))
    tok_ref[:, 3 * CH :] = last.astype(BF16)
    mine = jnp.zeros((128, 128), F32)
    for r in range(SLOTS):
        mine = mine + jnp.where(rank == r, p_ref[:, 0, r : r + 1], 0.0)
    gates = gate_ref[...].astype(F32)
    experts = iota((128, 128), 0)
    for k in range(4):
        total = jnp.sum(jnp.where(ids[k : k + 1, :] == experts, mine, 0.0), axis=0, keepdims=True)
        gate_out_ref[k : k + 1, :] = (total / gates[k : k + 1, :]).astype(BF16)


def ring_step(i):
    return jnp.where(i % 2 == 1, (i + 1) // 2, 8 - i // 2)


class Exchange:
    def __init__(self, route, src, mid, dst, send1, recv1, send2, recv2):
        self.route, self.src, self.mid, self.dst = route, src, mid, dst
        self.send1, self.recv1, self.send2, self.recv2 = send1, recv1, send2, recv2
        self.dp, me = lax.axis_index("dp"), lax.axis_index("expert")
        self.z, self.y, self.c = me // 16, (me // 2) % 8, me % 2

    def slab(self, p):
        return self.src.at[p] if self.route == "z" else self.src.at[:, p]

    def landing(self):
        return self.dst.at[:, self.y, self.c] if self.route == "z" else self.dst.at[self.z, :, self.c]

    def peer(self, p, c):
        return p * 16 + self.y * 2 + c, self.z * 16 + p * 2 + c

    def copy1(self, i):
        along = self.z if self.route == "z" else self.y
        p = (along + ring_step(i)) % 8
        by_z, by_y = self.peer(p, self.c)
        return pltpu.make_async_remote_copy(
            src_ref=self.slab(p),
            dst_ref=self.mid.at[along],
            send_sem=self.send1.at[i],
            recv_sem=self.recv1,
            device_id=(self.dp, by_z if self.route == "z" else by_y),
            device_id_type=pl.DeviceIdType.MESH,
        )

    def copy2(self, i):
        across = self.y if self.route == "z" else self.z
        p = (across + jnp.where(i < 14, ring_step(i // 2 + 1), 0)) % 8
        c = jnp.where(i < 14, i % 2, 1 - self.c)
        by_z, by_y = self.peer(p, c)
        return pltpu.make_async_remote_copy(
            src_ref=self.mid.at[:, p, c],
            dst_ref=self.landing(),
            send_sem=self.send2.at[i],
            recv_sem=self.recv2,
            device_id=(self.dp, by_y if self.route == "z" else by_z),
            device_id_type=pl.DeviceIdType.MESH,
        )

    def phase1(self):
        def one(i, _):
            self.copy1(i).start()
            return 0

        lax.fori_loop(1, 8, one, 0)
        along = self.z if self.route == "z" else self.y
        pltpu.make_async_copy(self.slab(along), self.mid.at[along], self.recv1).start()

    def phase2(self):
        pltpu.make_async_copy(self.mid, self.mid, self.recv1).wait()

        def one(i, _):
            self.copy2(i).start()
            return 0

        lax.fori_loop(0, 15, one, 0)
        across = self.y if self.route == "z" else self.z
        pltpu.make_async_copy(self.mid.at[:, across, self.c], self.landing(), self.recv2).start()

    def arrived(self):
        pltpu.make_async_copy(self.dst, self.dst, self.recv2).wait()

    def sent(self):
        def one(i, _):
            self.copy1(i).wait_send()
            return 0

        lax.fori_loop(1, 8, one, 0)

        def two(i, _):
            self.copy2(i).wait_send()
            return 0

        lax.fori_loop(0, 15, two, 0)


def greet(with_dp):
    dp, me = lax.axis_index("dp"), lax.axis_index("expert")
    z, y, c = me // 16, (me // 2) % 8, me % 2
    barrier = pltpu.get_barrier_semaphore()

    def signal(i, target):
        pl.semaphore_signal(barrier, inc=1, device_id=target, device_id_type=pl.DeviceIdType.MESH)

    def rings(i, _):
        for core in (c, 1 - c):
            signal(i, (dp, ((z + i) % 8) * 16 + y * 2 + core))
            signal(i, (dp, z * 16 + ((y + i) % 8) * 2 + core))
        return 0

    lax.fori_loop(1, 8, rings, 0)
    signal(0, (dp, z * 16 + y * 2 + 1 - c))
    if with_dp:
        for i in range(1, 4):
            signal(i, ((dp + i) % 4, me))
    pl.semaphore_wait(barrier, 32 if with_dp else 29)


def exchange_kernel(routes, scatter, *refs):
    n = len(routes)
    refs = list(refs)
    take = lambda count: [refs.pop(0) for _ in range(count)]
    srcs, parts = take(n), take(scatter)
    dsts, lands = take(n), take(scatter)
    mids = take(n)
    send1, recv1, send2, recv2, send3, recv3 = take(6)
    dp, me = lax.axis_index("dp"), lax.axis_index("expert")
    greet(scatter > 0)
    streams = [
        Exchange(
            routes[i], srcs[i], mids[i], dsts[i], send1.at[i], recv1.at[i], send2.at[i], recv2.at[i]
        )
        for i in range(n)
    ]
    for stream in streams:
        stream.phase1()

    def scatter_copy(k, i):
        target = (dp + i) % 4
        return pltpu.make_async_remote_copy(
            src_ref=parts[k].at[target],
            dst_ref=lands[k].at[dp],
            send_sem=send3.at[k, i],
            recv_sem=recv3.at[k],
            device_id=(target, me),
            device_id_type=pl.DeviceIdType.MESH,
        )

    for k in range(scatter):
        for i in (1, 3, 2):
            scatter_copy(k, i).start()
        pltpu.make_async_copy(parts[k].at[dp], lands[k].at[dp], recv3.at[k]).start()
    for stream in streams:
        stream.phase2()
    for stream in streams:
        stream.arrived()
    for stream in streams:
        stream.sent()
    for k in range(scatter):
        pltpu.make_async_copy(lands[k], lands[k], recv3.at[k]).wait()
        for i in (1, 3, 2):
            scatter_copy(k, i).wait_send()


def exchange(routes, arrays, parts, collective_id, name):
    n = len(arrays)
    wide = [a.reshape(8, 8, 2, *a.shape[1:]) for a in arrays]
    like = [jax.ShapeDtypeStruct(a.shape, a.dtype) for a in wide + list(parts)]
    sem = pltpu.SemaphoreType.DMA
    outs = pl.pallas_call(
        functools.partial(exchange_kernel, routes, len(parts)),
        out_shape=like,
        in_specs=[VMEM] * len(like),
        out_specs=[VMEM] * len(like),
        scratch_shapes=[pltpu.VMEM(a.shape, a.dtype) for a in wide]
        + [sem((n, 8)), sem((n,)), sem((n, 16)), sem((n,)), sem((3, 4)), sem((3,))],
        compiler_params=pltpu.CompilerParams(
            collective_id=collective_id, has_side_effects=True, vmem_limit_bytes=24 << 20
        ),
        name=name,
    )(*wide, *parts)
    return [o.reshape(128, *o.shape[3:]) for o in outs[:n]], outs[n:]


def local(kernel, out_shape, args, scratch=(), name=None):
    return pl.pallas_call(
        kernel,
        out_shape=out_shape,
        in_specs=[VMEM] * len(args),
        out_specs=jax.tree.map(lambda _: VMEM, out_shape),
        scratch_shapes=scratch,
        compiler_params=pltpu.CompilerParams(vmem_limit_bytes=48 << 20),
        name=name,
    )(*args)


def shape(*dims, dtype=BF16):
    return jax.ShapeDtypeStruct(dims, dtype)


def shards(tokens, grad_out, expert_ids, gate_weight, w_gate, w_up, w_down):
    ids, gates = expert_ids.T, gate_weight.T
    half = shape(128, BLOCK, 384)
    send = local(pack_kernel, (half,) * 4, (ids, gates, tokens, grad_out), name="pack")
    got, _ = exchange(("z", "y", "z", "y"), send, [], 0, "dispatch")
    *back, part_gate, part_up, part_down = local(
        compute_kernel,
        (half, half, shape(128, 1, 128, dtype=F32))
        + (shape(4, 256, 384), shape(4, 256, 384), shape(4, 384, 256)),
        (*got, w_gate[0], w_up[0], w_down[0]),
        scratch=[
            pltpu.VMEM((ROWS, 1024), BF16),
            pltpu.VMEM((ROWS, 1024), BF16),
            pltpu.VMEM((ROWS, 384), BF16),
            pltpu.VMEM((ROWS, 384), BF16),
            pltpu.VMEM((ROWS, 384), BF16),
        ],
        name="compute",
    )
    home, sums = exchange(("z", "y", "z"), back, [part_gate, part_up, part_down], 1, "return")
    wide = shape(1, 256, 384, dtype=F32)
    grad_tokens, grad_gate, *grads = local(
        combine_kernel,
        (shape(128, 1024), shape(4, 128), wide, wide, shape(1, 384, 256, dtype=F32)),
        (ids, gates, *home, *sums),
        name="combine",
    )
    return (grad_tokens, grad_gate.T, *grads)


def solution(mesh):
    rows = P(("dp", "expert"), None)
    weights = P("expert", None, None)
    return jax.shard_map(
        shards,
        mesh=mesh,
        in_specs=(rows, rows, rows, rows, weights, weights, weights),
        out_specs=(rows, rows, P("expert", "dp", None), P("expert", "dp", None), P("expert", None, "dp")),
        check_vma=False,
    )
```

```python
import functools

import jax
import jax.numpy as jnp
from jax import lax
from jax.experimental import pallas as pl
from jax.experimental.pallas import tpu as pltpu
from jax.sharding import PartitionSpec as P

F32, BF16 = jnp.float32, jnp.bfloat16
SLOTS = 6
BLOCK = 8
ROWS = 1024
CH = 256
VMEM = pl.BlockSpec(memory_space=pltpu.VMEM)


def dot(a, b, contract=((1,), (0,))):
    return lax.dot_general(a, b, (contract, ((), ())), preferred_element_type=F32)


def iota(shape, dim):
    return lax.broadcasted_iota(jnp.int32, shape, dim)


def one_hots(ids):
    experts = iota((128, 128), 0)
    named = jnp.zeros((128, 128), F32)
    for k in range(4):
        named = named + jnp.where(ids[k : k + 1, :] == experts, 1.0, 0.0)
    named = named.astype(BF16)
    earlier = jnp.where(iota((128, 128), 0) < iota((128, 128), 1), 1.0, 0.0).astype(BF16)
    rank = dot(named, earlier)
    rank = jnp.where(named.astype(F32) > 0.5, rank, -1.0)
    spread = jnp.where(iota((ROWS, 128), 0) // BLOCK == iota((ROWS, 128), 1), 1.0, 0.0).astype(BF16)
    ranks = dot(spread, rank.astype(BF16))
    place = (iota((ROWS, 128), 0) % BLOCK).astype(F32)
    main = jnp.where((ranks == place) & (place < 5.5), 1.0, 0.0)
    tails = [
        jnp.where((ranks == 3.0 * (place - 6.0) + j) & (place > 5.5), 1.0, 0.0) for j in range(3)
    ]
    return rank, main, tails, spread


def put_chunk(halves, blocks, j, rows):
    low, high = halves
    lead = low.at[blocks].shape[:-1]

    def put(ref, at, value):
        ref[(blocks, *[slice(None)] * (len(lead) - 1), at)] = value.reshape(*lead, value.shape[1])

    if j == 0:
        put(low, slice(0, 256), rows)
    elif j == 1:
        put(low, slice(256, 384), rows[:, 0:128])
        put(high, slice(0, 128), rows[:, 128:256])
    else:
        put(high, slice(128, 384), rows)


def get_chunk(halves, blocks, j):
    low, high = halves

    def get(ref, lo, hi):
        at = (blocks, *[slice(None)] * (len(ref.shape) - 2), slice(lo, hi))
        return ref[at].reshape(-1, hi - lo)

    if j == 0:
        return get(low, 0, 256)
    if j == 1:
        return jnp.concatenate([get(low, 256, 384), get(high, 0, 128)], axis=1)
    return get(high, 128, 384)


def pack_kernel(ids_ref, gate_ref, tok_ref, up_ref, xa_ref, xb_ref, sa_ref, sb_ref):
    ids = ids_ref[...]
    _, main, tails, spread = one_hots(ids)
    gates = gate_ref[...].astype(F32)
    experts = iota((128, 128), 0)
    gate_of = jnp.zeros((128, 128), F32)
    for k in range(4):
        gate_of = gate_of + jnp.where(ids[k : k + 1, :] == experts, gates[k : k + 1, :], 0.0)
    gate_rows = dot(spread, gate_of.astype(BF16))
    for j in range(3):
        gate_col = jnp.sum((main + tails[j]) * gate_rows, axis=1, keepdims=True)
        pick = jnp.concatenate([main.astype(BF16), tails[j].astype(BF16)], axis=1)
        for which, ref in enumerate((tok_ref, up_ref)):
            both = jnp.concatenate(
                [ref[:, j * CH : (j + 1) * CH], ref[:, 3 * CH : 4 * CH]], axis=0
            )
            rows = dot(pick, both)
            if which == 1:
                rows = rows * gate_col
            halves = ((xa_ref, xb_ref), (sa_ref, sb_ref))[which]
            put_chunk(halves, slice(None), j, rows.astype(BF16))


def combine_kernel(
    ids_ref, gate_ref, ba_ref, bb_ref, p_ref, rg_ref, ru_ref, rd_ref,
    tok_ref, gate_out_ref, gg_ref, gu_ref, gd_ref
):
    for part, total in ((rg_ref, gg_ref), (ru_ref, gu_ref), (rd_ref, gd_ref)):
        total[0] = sum(part[i].astype(F32) for i in range(1, 4)) + part[0].astype(F32)
    ids = ids_ref[...]
    rank, main, tails, _ = one_hots(ids)
    main = main.astype(BF16)
    last = jnp.zeros((128, CH), F32)
    for j in range(3):
        part = get_chunk((ba_ref, bb_ref), slice(None), j)
        tok_ref[:, j * CH : (j + 1) * CH] = dot(main, part, ((0,), (0,))).astype(BF16)
        last = last + dot(tails[j].astype(BF16), part, ((0,), (0,)))
    tok_ref[:, 3 * CH :] = last.astype(BF16)
    mine = jnp.zeros((128, 128), F32)
    for r in range(SLOTS):
        mine = mine + jnp.where(rank == r, p_ref[:, 0, r : r + 1], 0.0)
    gates = gate_ref[...].astype(F32)
    experts = iota((128, 128), 0)
    for k in range(4):
        total = jnp.sum(jnp.where(ids[k : k + 1, :] == experts, mine, 0.0), axis=0, keepdims=True)
        gate_out_ref[k : k + 1, :] = (total / gates[k : k + 1, :]).astype(BF16)


def ring_step(i):
    return jnp.where(i % 2 == 1, (i + 1) // 2, 8 - i // 2)


class Exchange:
    def __init__(self, route, src, mid, dst, send1, recv1, send2, recv2):
        self.route, self.src, self.mid, self.dst = route, src, mid, dst
        self.send1, self.recv1, self.send2, self.recv2 = send1, recv1, send2, recv2
        self.dp, me = lax.axis_index("dp"), lax.axis_index("expert")
        self.z, self.y, self.c = me // 16, (me // 2) % 8, me % 2

    def slab(self, p):
        return self.src.at[p] if self.route == "z" else self.src.at[:, p]

    def landing(self):
        return self.dst.at[:, self.y, self.c] if self.route == "z" else self.dst.at[self.z, :, self.c]

    def peer(self, p, c):
        return p * 16 + self.y * 2 + c, self.z * 16 + p * 2 + c

    def along(self):
        return self.z if self.route == "z" else self.y

    def first(self, p):
        by_z, by_y = self.peer(p, self.c)
        return by_z if self.route == "z" else by_y

    def copy1(self, p):
        return pltpu.make_async_remote_copy(
            src_ref=self.slab(p),
            dst_ref=self.mid.at[self.along()],
            send_sem=self.send1.at[p],
            recv_sem=self.recv1,
            device_id=(self.dp, self.first(p)),
            device_id_type=pl.DeviceIdType.MESH,
        )

    def piece1(self, p, g):
        zs = pl.ds(2 * g, 2)
        return pltpu.make_async_remote_copy(
            src_ref=self.src.at[zs, p],
            dst_ref=self.mid.at[self.y, zs],
            send_sem=self.send1.at[8 * g + p],
            recv_sem=self.recv1,
            device_id=(self.dp, self.first(p)),
            device_id_type=pl.DeviceIdType.MESH,
        )

    def group1(self, g):
        if self.route == "z":
            for p in (2 * g, 2 * g + 1):

                @pl.when(p != self.z)
                def _():
                    self.copy1(p).start()

                @pl.when(p == self.z)
                def _():
                    pltpu.make_async_copy(self.slab(p), self.mid.at[p], self.recv1).start()

        else:

            def one(i, _):
                self.piece1((self.y + ring_step(i)) % 8, g).start()
                return 0

            lax.fori_loop(1, 8, one, 0)
            zs = pl.ds(2 * g, 2)
            pltpu.make_async_copy(
                self.src.at[zs, self.y], self.mid.at[self.y, zs], self.recv1
            ).start()

    def copy2(self, i):
        across = self.y if self.route == "z" else self.z
        p = (across + jnp.where(i < 14, ring_step(i // 2 + 1), 0)) % 8
        c = jnp.where(i < 14, i % 2, 1 - self.c)
        by_z, by_y = self.peer(p, c)
        return pltpu.make_async_remote_copy(
            src_ref=self.mid.at[:, p, c],
            dst_ref=self.landing(),
            send_sem=self.send2.at[i],
            recv_sem=self.recv2,
            device_id=(self.dp, by_y if self.route == "z" else by_z),
            device_id_type=pl.DeviceIdType.MESH,
        )

    def phase1(self):
        along = self.along()

        def one(i, _):
            self.copy1((along + ring_step(i)) % 8).start()
            return 0

        lax.fori_loop(1, 8, one, 0)
        pltpu.make_async_copy(self.slab(along), self.mid.at[along], self.recv1).start()

    def phase2(self):
        pltpu.make_async_copy(self.mid, self.mid, self.recv1).wait()

        def one(i, _):
            self.copy2(i).start()
            return 0

        lax.fori_loop(0, 15, one, 0)
        across = self.y if self.route == "z" else self.z
        pltpu.make_async_copy(self.mid.at[:, across, self.c], self.landing(), self.recv2).start()

    def arrived(self):
        pltpu.make_async_copy(self.dst, self.dst, self.recv2).wait()

    def sent(self, grouped=False):
        def one(i, _):
            p = (self.along() + i) % 8
            if grouped and self.route == "y":
                for g in range(4):
                    self.piece1(p, g).wait_send()
            else:
                self.copy1(p).wait_send()
            return 0

        lax.fori_loop(1, 8, one, 0)

        def two(i, _):
            self.copy2(i).wait_send()
            return 0

        lax.fori_loop(0, 15, two, 0)


def greet():
    dp, me = lax.axis_index("dp"), lax.axis_index("expert")
    z, y, c = me // 16, (me // 2) % 8, me % 2
    barrier = pltpu.get_barrier_semaphore()

    def signal(target):
        pl.semaphore_signal(barrier, inc=1, device_id=target, device_id_type=pl.DeviceIdType.MESH)

    def rings(i, _):
        for core in (c, 1 - c):
            signal((dp, ((z + i) % 8) * 16 + y * 2 + core))
            signal((dp, z * 16 + ((y + i) % 8) * 2 + core))
        return 0

    lax.fori_loop(1, 8, rings, 0)
    signal((dp, z * 16 + y * 2 + 1 - c))
    for i in range(1, 4):
        signal(((dp + i) % 4, me))
    pl.semaphore_wait(barrier, 32)


def main_kernel(*refs):
    refs = list(refs)
    take = lambda count: [refs.pop(0) for _ in range(count)]
    sends, weights_hbm = take(4), take(3)
    homes, lands = take(3), take(3)
    mids, gots, weights = take(4), take(4), take(3)
    x_s, s_s, a_s, silu_s, dg_s, du_s, h_s = take(7)
    backs, back_mids, parts = take(3), take(3), take(3)
    send1, recv1, send2, recv2, send3, recv3, load = take(7)
    dp, me = lax.axis_index("dp"), lax.axis_index("expert")
    loads = [pltpu.make_async_copy(weights_hbm[i], weights[i], load.at[i]) for i in range(3)]
    for one in loads:
        one.start()
    greet()
    outward = [
        Exchange(
            "zyzy"[i], sends[i], mids[i], gots[i], send1.at[i], recv1.at[i], send2.at[i], recv2.at[i]
        )
        for i in range(4)
    ]
    homeward = [
        Exchange(
            "zyz"[i], backs[i], back_mids[i], homes[i],
            send1.at[4 + i], recv1.at[4 + i], send2.at[4 + i], recv2.at[4 + i],
        )
        for i in range(3)
    ]
    for stream in outward:
        stream.phase1()
    for stream in outward:
        stream.phase2()

    row, col = iota((CH, CH), 0), iota((CH, CH), 1)
    same = row // BLOCK == col // BLOCK
    ra, ca = row % BLOCK, col % BLOCK
    unpack = jnp.concatenate(
        [
            jnp.where(same & (ra < 6) & (ca == 6 + ra // 3) & (ra % 3 == j), 1.0, 0.0)
            for j in range(3)
        ],
        axis=1,
    ).astype(BF16)
    repack = [
        jnp.where(same & (ra >= 6) & (ca == 3 * (ra - 6) + j), 1.0, 0.0).astype(BF16)
        for j in range(3)
    ]
    real = (iota((CH, 1), 0) % BLOCK) < SLOTS
    spot = iota((CH, 128), 1) == iota((CH, 128), 0) % BLOCK
    wg, wu, wd = weights

    def rows_of(g):
        return pl.ds(pl.multiple_of(g * CH, CH), CH)

    def unpack_group(halves, ref, g):
        rows = rows_of(g)
        chunks = []
        for j in range(3):
            chunk = get_chunk(halves, pl.ds(2 * g, 2), j)
            ref[rows, j * CH : (j + 1) * CH] = chunk
            chunks.append(chunk)
        ref[rows, 3 * CH :] = dot(unpack, jnp.concatenate(chunks, axis=0)).astype(BF16)

    for one in loads:
        one.wait()
    for stream in outward[:2]:
        stream.arrived()

    def forward(g, _):
        rows = rows_of(g)
        unpack_group(gots[:2], x_s, g)
        x = x_s[rows, :]
        pre_gate = dot(x, wg[...])
        pre_up = dot(x, wu[...])
        sig = jax.nn.sigmoid(pre_gate)
        silu = jnp.where(real, pre_gate * sig, 0.0)
        h_s[rows, :] = (silu * pre_up).astype(BF16)
        silu_s[rows, :] = silu
        a_s[rows, :] = jnp.where(real, pre_up * sig * (1.0 + pre_gate * (1.0 - sig)), 0.0)
        return 0

    lax.fori_loop(0, 4, forward, 0)
    for stream in outward[2:]:
        stream.arrived()

    def backward(g, _):
        rows = rows_of(g)
        zs = pl.ds(2 * g, 2)
        unpack_group(gots[2:], s_s, g)
        hgrad = dot(s_s[rows, :], wd[...], ((1,), (1,)))
        d_gate = (hgrad * a_s[rows, :]).astype(BF16)
        d_up = (hgrad * silu_s[rows, :]).astype(BF16)
        dg_s[rows, :] = d_gate
        du_s[rows, :] = d_up
        product = jnp.sum(h_s[rows, :].astype(F32) * hgrad, axis=1, keepdims=True)
        spots = jnp.where(spot, product, 0.0).reshape(CH // BLOCK, BLOCK, 128)
        backs[2][zs] = jnp.sum(spots, axis=1).reshape(2, 8, 2, 1, 128)

        def route(cols):
            return dot(d_gate, wg[cols, :], ((1,), (1,))) + dot(d_up, wu[cols, :], ((1,), (1,)))

        tail = route(slice(3 * CH, 4 * CH)).astype(BF16)
        for j in range(3):
            part = route(slice(j * CH, (j + 1) * CH)) + dot(repack[j], tail)
            put_chunk(backs[:2], zs, j, part.astype(BF16))

        @pl.when(g > 0)
        def _():
            for stream in homeward:
                stream.group1(g - 1)

        return 0

    lax.fori_loop(0, 4, backward, 0)

    def grads(i, _):
        cols = pl.ds(pl.multiple_of(i * CH, CH), CH)
        x = x_s[:, cols]
        parts[0][i] = dot(x, dg_s[...], ((0,), (0,))).astype(BF16)
        parts[1][i] = dot(x, du_s[...], ((0,), (0,))).astype(BF16)
        parts[2][i] = dot(h_s[...], s_s[:, cols], ((0,), (0,))).astype(BF16)
        return 0

    lax.fori_loop(0, 4, grads, 0)
    for stream in homeward:
        stream.group1(3)

    def scatter_copy(k, i):
        target = (dp + i) % 4
        return pltpu.make_async_remote_copy(
            src_ref=parts[k].at[target],
            dst_ref=lands[k].at[dp],
            send_sem=send3.at[k, i],
            recv_sem=recv3.at[k],
            device_id=(target, me),
            device_id_type=pl.DeviceIdType.MESH,
        )

    for k in range(3):
        for i in (1, 3, 2):
            scatter_copy(k, i).start()
        pltpu.make_async_copy(parts[k].at[dp], lands[k].at[dp], recv3.at[k]).start()
    for stream in homeward:
        stream.phase2()
    for stream in homeward:
        stream.arrived()
    for stream in outward:
        stream.sent()
    for stream in homeward:
        stream.sent(grouped=True)
    for k in range(3):
        pltpu.make_async_copy(lands[k], lands[k], recv3.at[k]).wait()
        for i in (1, 3, 2):
            scatter_copy(k, i).wait_send()


def local(kernel, out_shape, args, scratch=(), name=None):
    return pl.pallas_call(
        kernel,
        out_shape=out_shape,
        in_specs=[VMEM] * len(args),
        out_specs=jax.tree.map(lambda _: VMEM, out_shape),
        scratch_shapes=scratch,
        compiler_params=pltpu.CompilerParams(vmem_limit_bytes=48 << 20),
        name=name,
    )(*args)


def shape(*dims, dtype=BF16):
    return jax.ShapeDtypeStruct(dims, dtype)


def shards(tokens, grad_out, expert_ids, gate_weight, w_gate, w_up, w_down):
    ids, gates = expert_ids.T, gate_weight.T
    send = local(pack_kernel, (shape(128, BLOCK, 384),) * 4, (ids, gates, tokens, grad_out), name="pack")
    half, small = (8, 8, 2, BLOCK, 384), (8, 8, 2, 1, 128)
    blocks = [(half, BF16), (half, BF16), (small, F32)]
    parts = [((4, 256, 384), BF16), ((4, 256, 384), BF16), ((4, 384, 256), BF16)]
    weights = [((1024, 384), BF16), ((1024, 384), BF16), ((384, 1024), BF16)]
    rows = [((ROWS, 1024), BF16)] * 2 + [((ROWS, 384), F32)] * 2 + [((ROWS, 384), BF16)] * 3
    sem = pltpu.SemaphoreType.DMA
    *home, land_gate, land_up, land_down = pl.pallas_call(
        main_kernel,
        out_shape=[shape(*dims, dtype=kind) for dims, kind in blocks + parts],
        in_specs=[VMEM] * 4 + [pl.BlockSpec(memory_space=pl.ANY)] * 3,
        out_specs=[VMEM] * 6,
        scratch_shapes=[
            pltpu.VMEM(dims, kind)
            for dims, kind in [(half, BF16)] * 8 + weights + rows + blocks * 2 + parts
        ]
        + [sem((7, 32)), sem((7,)), sem((7, 16)), sem((7,)), sem((3, 4)), sem((3,)), sem((3,))],
        compiler_params=pltpu.CompilerParams(
            collective_id=0, has_side_effects=True, vmem_limit_bytes=50 << 20
        ),
        name="main",
    )(*[a.reshape(half) for a in send], w_gate[0], w_up[0], w_down[0])
    home = [a.reshape(128, *a.shape[3:]) for a in home]
    sums = (land_gate, land_up, land_down)
    wide = shape(1, 256, 384, dtype=F32)
    grad_tokens, grad_gate, *grads = local(
        combine_kernel,
        (shape(128, 1024), shape(4, 128), wide, wide, shape(1, 384, 256, dtype=F32)),
        (ids, gates, *home, *sums),
        name="combine",
    )
    return (grad_tokens, grad_gate.T, *grads)


def solution(mesh):
    rows = P(("dp", "expert"), None)
    weights = P("expert", None, None)
    return jax.shard_map(
        shards,
        mesh=mesh,
        in_specs=(rows, rows, rows, rows, weights, weights, weights),
        out_specs=(rows, rows, P("expert", "dp", None), P("expert", "dp", None), P("expert", None, "dp")),
        check_vma=False,
    )
```

```python
import functools

import jax
import jax.numpy as jnp
from jax import lax
from jax.experimental import pallas as pl
from jax.experimental.pallas import tpu as pltpu
from jax.sharding import PartitionSpec as P

F32, BF16 = jnp.float32, jnp.bfloat16
SLOTS = 6
BLOCK = 8
ROWS = 1024
CH = 256
VMEM = pl.BlockSpec(memory_space=pltpu.VMEM)


def dot(a, b, contract=((1,), (0,))):
    return lax.dot_general(a, b, (contract, ((), ())), preferred_element_type=F32)


def iota(shape, dim):
    return lax.broadcasted_iota(jnp.int32, shape, dim)


def one_hots(ids):
    experts = iota((128, 128), 0)
    named = jnp.zeros((128, 128), F32)
    for k in range(4):
        named = named + jnp.where(ids[k : k + 1, :] == experts, 1.0, 0.0)
    named = named.astype(BF16)
    earlier = jnp.where(iota((128, 128), 0) < iota((128, 128), 1), 1.0, 0.0).astype(BF16)
    rank = dot(named, earlier)
    rank = jnp.where(named.astype(F32) > 0.5, rank, -1.0)
    spread = jnp.where(iota((ROWS, 128), 0) // BLOCK == iota((ROWS, 128), 1), 1.0, 0.0).astype(BF16)
    ranks = dot(spread, rank.astype(BF16))
    place = (iota((ROWS, 128), 0) % BLOCK).astype(F32)
    main = jnp.where((ranks == place) & (place < 5.5), 1.0, 0.0)
    tails = [
        jnp.where((ranks == 3.0 * (place - 6.0) + j) & (place > 5.5), 1.0, 0.0) for j in range(3)
    ]
    return rank, main, tails, spread


def put_chunk(halves, blocks, j, rows):
    low, high = halves
    lead = low.at[blocks].shape[:-1]

    def put(ref, at, value):
        ref[(blocks, *[slice(None)] * (len(lead) - 1), at)] = value.reshape(*lead, value.shape[1])

    if j == 0:
        put(low, slice(0, 256), rows)
    elif j == 1:
        put(low, slice(256, 384), rows[:, 0:128])
        put(high, slice(0, 128), rows[:, 128:256])
    else:
        put(high, slice(128, 384), rows)


def get_chunk(halves, blocks, j):
    low, high = halves

    def get(ref, lo, hi):
        at = (blocks, *[slice(None)] * (len(ref.shape) - 2), slice(lo, hi))
        return ref[at].reshape(-1, hi - lo)

    if j == 0:
        return get(low, 0, 256)
    if j == 1:
        return jnp.concatenate([get(low, 256, 384), get(high, 0, 128)], axis=1)
    return get(high, 128, 384)


def combine_kernel(
    ids_ref, gate_ref, ba_ref, bb_ref, p_ref, rg_ref, ru_ref, rd_ref,
    tok_ref, gate_out_ref, gg_ref, gu_ref, gd_ref
):
    for part, total in ((rg_ref, gg_ref), (ru_ref, gu_ref), (rd_ref, gd_ref)):
        total[0] = sum(part[i].astype(F32) for i in range(1, 4)) + part[0].astype(F32)
    ids = ids_ref[...]
    rank, main, tails, _ = one_hots(ids)
    main = main.astype(BF16)
    last = jnp.zeros((128, CH), F32)
    for j in range(3):
        part = get_chunk((ba_ref, bb_ref), slice(None), j)
        tok_ref[:, j * CH : (j + 1) * CH] = dot(main, part, ((0,), (0,))).astype(BF16)
        last = last + dot(tails[j].astype(BF16), part, ((0,), (0,)))
    tok_ref[:, 3 * CH :] = last.astype(BF16)
    mine = jnp.zeros((128, 128), F32)
    for r in range(SLOTS):
        mine = mine + jnp.where(rank == r, p_ref[:, 0, r : r + 1], 0.0)
    gates = gate_ref[...].astype(F32)
    experts = iota((128, 128), 0)
    for k in range(4):
        total = jnp.sum(jnp.where(ids[k : k + 1, :] == experts, mine, 0.0), axis=0, keepdims=True)
        gate_out_ref[k : k + 1, :] = (total / gates[k : k + 1, :]).astype(BF16)


def ring_step(i):
    return jnp.where(i % 2 == 1, (i + 1) // 2, 8 - i // 2)


class Exchange:
    def __init__(self, route, src, mid, dst, send1, recv1, send2, recv2):
        self.route, self.src, self.mid, self.dst = route, src, mid, dst
        self.send1, self.recv1, self.send2, self.recv2 = send1, recv1, send2, recv2
        self.dp, me = lax.axis_index("dp"), lax.axis_index("expert")
        self.z, self.y, self.c = me // 16, (me // 2) % 8, me % 2

    def slab(self, p):
        return self.src.at[p] if self.route == "z" else self.src.at[:, p]

    def landing(self):
        return self.dst.at[:, self.y, self.c] if self.route == "z" else self.dst.at[self.z, :, self.c]

    def peer(self, p, c):
        return p * 16 + self.y * 2 + c, self.z * 16 + p * 2 + c

    def along(self):
        return self.z if self.route == "z" else self.y

    def first(self, p):
        by_z, by_y = self.peer(p, self.c)
        return by_z if self.route == "z" else by_y

    def copy1(self, p):
        return pltpu.make_async_remote_copy(
            src_ref=self.slab(p),
            dst_ref=self.mid.at[self.along()],
            send_sem=self.send1.at[p],
            recv_sem=self.recv1,
            device_id=(self.dp, self.first(p)),
            device_id_type=pl.DeviceIdType.MESH,
        )

    def piece1(self, p, g):
        zs = pl.ds(2 * g, 2)
        return pltpu.make_async_remote_copy(
            src_ref=self.src.at[zs, p],
            dst_ref=self.mid.at[self.y, zs],
            send_sem=self.send1.at[8 * g + p],
            recv_sem=self.recv1,
            device_id=(self.dp, self.first(p)),
            device_id_type=pl.DeviceIdType.MESH,
        )

    def group1(self, g):
        if self.route == "z":
            for p in (2 * g, 2 * g + 1):

                @pl.when(p != self.z)
                def _():
                    self.copy1(p).start()

                @pl.when(p == self.z)
                def _():
                    pltpu.make_async_copy(self.slab(p), self.mid.at[p], self.recv1).start()

        else:

            def one(i, _):
                self.piece1((self.y + ring_step(i)) % 8, g).start()
                return 0

            lax.fori_loop(1, 8, one, 0)
            zs = pl.ds(2 * g, 2)
            pltpu.make_async_copy(
                self.src.at[zs, self.y], self.mid.at[self.y, zs], self.recv1
            ).start()

    def copy2(self, i):
        across = self.y if self.route == "z" else self.z
        p = (across + jnp.where(i < 14, ring_step(i // 2 + 1), 0)) % 8
        c = jnp.where(i < 14, i % 2, 1 - self.c)
        by_z, by_y = self.peer(p, c)
        return pltpu.make_async_remote_copy(
            src_ref=self.mid.at[:, p, c],
            dst_ref=self.landing(),
            send_sem=self.send2.at[i],
            recv_sem=self.recv2,
            device_id=(self.dp, by_y if self.route == "z" else by_z),
            device_id_type=pl.DeviceIdType.MESH,
        )

    def phase2(self, received=True):
        if received:
            pltpu.make_async_copy(self.mid, self.mid, self.recv1).wait()

        def one(i, _):
            self.copy2(i).start()
            return 0

        lax.fori_loop(0, 15, one, 0)
        across = self.y if self.route == "z" else self.z
        pltpu.make_async_copy(self.mid.at[:, across, self.c], self.landing(), self.recv2).start()

    def arrived(self):
        pltpu.make_async_copy(self.dst, self.dst, self.recv2).wait()

    def sent1(self):
        def one(i, _):
            p = (self.along() + i) % 8
            if self.route == "y":
                for g in range(4):
                    self.piece1(p, g).wait_send()
            else:
                self.copy1(p).wait_send()
            return 0

        lax.fori_loop(1, 8, one, 0)

    def sent2(self):
        def two(i, _):
            self.copy2(i).wait_send()
            return 0

        lax.fori_loop(0, 15, two, 0)


def greet():
    dp, me = lax.axis_index("dp"), lax.axis_index("expert")
    z, y, c = me // 16, (me // 2) % 8, me % 2
    barrier = pltpu.get_barrier_semaphore()

    def signal(target):
        pl.semaphore_signal(barrier, inc=1, device_id=target, device_id_type=pl.DeviceIdType.MESH)

    def rings(i, _):
        for core in (c, 1 - c):
            signal((dp, ((z + i) % 8) * 16 + y * 2 + core))
            signal((dp, z * 16 + ((y + i) % 8) * 2 + core))
        return 0

    lax.fori_loop(1, 8, rings, 0)
    signal((dp, z * 16 + y * 2 + 1 - c))
    for i in range(1, 4):
        signal(((dp + i) % 4, me))
    return barrier


class Ring:
    def __init__(self, number, inputs, ids, gates, held, held_ids, held_gates, xs, ss, send, recv, few, meta):
        self.number, self.inputs, self.ids, self.gates = number, inputs, ids, gates
        self.held, self.held_ids, self.held_gates = held, held_ids, held_gates
        self.xs, self.ss, self.send, self.recv, self.few, self.meta = xs, ss, send, recv, few, meta
        self.dp, me = lax.axis_index("dp"), lax.axis_index("expert")
        self.z, self.y, self.c = me // 16, (me // 2) % 8, me % 2
        self.at = self.y if number else self.z

    def device(self, p):
        if self.number:
            return (self.dp, self.z * 16 + p * 2 + self.c)
        return (self.dp, p * 16 + self.y * 2 + self.c)

    def own(self, part):
        return self.inputs[part].at[:, pl.ds(512 * self.number, 512)]

    def copy(self, part, way, step):
        block = (self.at - way * (step - 1) + 8) % 8
        which = part * 2 + (way > 0)
        return pltpu.make_async_remote_copy(
            src_ref=self.own(part) if step == 1 else self.held.at[block, part],
            dst_ref=self.held.at[block, part],
            send_sem=self.send.at[which, step],
            recv_sem=self.recv.at[which, step],
            device_id=self.device((self.at + way + 8) % 8),
            device_id_type=pl.DeviceIdType.MESH,
        )

    def arrived(self, part, way, step):
        block = self.held.at[(self.at - way * step + 8) % 8, part]
        pltpu.make_async_copy(block, block, self.recv.at[part * 2 + (way > 0), step]).wait()

    def small(self, i):
        for k, (src, dst) in enumerate(((self.ids, self.held_ids), (self.gates, self.held_gates))):
            yield pltpu.make_async_remote_copy(
                src_ref=src,
                dst_ref=dst.at[self.at],
                send_sem=self.few.at[k, i],
                recv_sem=self.meta.at[k],
                device_id=self.device((self.at + i) % 8),
                device_id_type=pl.DeviceIdType.MESH,
            )

    def pick(self, block, ids, gates):
        row = iota((128, 128), 0)
        place, receiver = (row % BLOCK).astype(F32), row // BLOCK
        if self.number:
            expert = receiver // 2 * 16 + self.y * 2 + receiver % 2
        else:
            expert = self.z * 16 + receiver
        named, gate = jnp.zeros((128, 128), F32), jnp.zeros((128, 128), F32)
        for k in range(4):
            hit = ids[k : k + 1, :] == expert
            named = jnp.where(hit, 1.0, named)
            gate = jnp.where(hit, gates[k : k + 1, :], gate)
        earlier = jnp.where(row < iota((128, 128), 1), 1.0, 0.0).astype(BF16)
        rank = jnp.where(named > 0.5, dot(named.astype(BF16), earlier), -1.0)
        main = jnp.where((rank == place) & (place < 5.5), 1.0, 0.0)
        held = self.held

        def chunk(j):
            return jnp.concatenate(
                [held[block, part, :, j * 128 : (j + 1) * 128] for part in range(2)], axis=1
            )

        last = chunk(3)
        for j in range(3):
            tail = jnp.where((rank == 3.0 * (place - 6.0) + j) & (place > 5.5), 1.0, 0.0)
            scale = jnp.sum((main + tail) * gate, axis=1, keepdims=True)
            choice = jnp.concatenate([main.astype(BF16), tail.astype(BF16)], axis=1)
            rows = dot(choice, jnp.concatenate([chunk(j), last], axis=0))
            lanes = slice(j * 128, (j + 1) * 128)
            self.xs[block, :, :, :, lanes] = rows[:, :128].astype(BF16).reshape(8, 2, 8, 128)
            self.ss[block, :, :, :, lanes] = (
                (rows[:, 128:] * scale).astype(BF16).reshape(8, 2, 8, 128)
            )

    def pick_step(self, way, step):
        block = (self.at - way * step + 8) % 8
        self.pick(block, self.held_ids[block], self.held_gates[block].astype(F32))


def main_kernel(*refs):
    refs = list(refs)
    take = lambda count: [refs.pop(0) for _ in range(count)]
    (ids, gates), inputs, weights_hbm = take(2), take(2), take(3)
    homes, lands = take(3), take(3)
    helds, held_ids, held_gates, (my_ids, my_gates) = take(2), take(2), take(2), take(2)
    mids, gots, weights = take(4), take(4), take(3)
    x_s, s_s, a_s, silu_s, dg_s, du_s, h_s = take(7)
    backs, back_mids, parts = take(3), take(3), take(3)
    send1, recv1, send2, recv2, send3, recv3, load = take(7)
    ring_send, ring_recv, few, meta, mine = take(5)
    barrier = greet()
    dp, me = lax.axis_index("dp"), lax.axis_index("expert")
    rings = [
        Ring(
            t, inputs, ids, gates, helds[t], held_ids[t], held_gates[t], mids[t], mids[2 + t],
            ring_send.at[t], ring_recv.at[t], few.at[t], meta.at[t],
        )
        for t in range(2)
    ]
    outward = [
        Exchange("zyzy"[i], None, mids[i], gots[i], None, None, send2.at[i], recv2.at[i])
        for i in range(4)
    ]
    homeward = [
        Exchange(
            "zyz"[i], backs[i], back_mids[i], homes[i],
            send1.at[i], recv1.at[i], send2.at[4 + i], recv2.at[4 + i],
        )
        for i in range(3)
    ]
    locals_ = [
        pltpu.make_async_copy(ids, my_ids, mine.at[0]),
        pltpu.make_async_copy(gates, my_gates, mine.at[1]),
    ] + [
        pltpu.make_async_copy(ring.own(part), ring.held.at[ring.at, part], mine.at[2 + 2 * t + part])
        for t, ring in enumerate(rings)
        for part in range(2)
    ]
    loads = [pltpu.make_async_copy(weights_hbm[i], weights[i], load.at[i]) for i in range(3)]
    for one in locals_ + loads:
        one.start()
    for ring in rings:
        pltpu.make_async_copy(ids, ring.held_ids.at[ring.at], ring.meta.at[0]).start()
        pltpu.make_async_copy(gates, ring.held_gates.at[ring.at], ring.meta.at[1]).start()
    for one in locals_:
        one.wait()
    for ring in rings:
        ring.pick(ring.at, my_ids[...], my_gates[...].astype(F32))
    pl.semaphore_wait(barrier, 32)
    for i in range(1, 8):
        for ring in rings:
            for one in ring.small(i):
                one.start()
    for part in range(2):
        for ring in rings:
            for way in (1, -1):
                ring.copy(part, way, 1).start()
    for ring in rings:
        pltpu.make_async_copy(ring.held_ids, ring.held_ids, ring.meta.at[0]).wait()
        pltpu.make_async_copy(ring.held_gates, ring.held_gates, ring.meta.at[1]).wait()
    for step in range(2, 5):
        for part in range(2):
            for ring in rings:
                for way in (1, -1):
                    ring.arrived(part, way, step - 1)
                    if step < 4 or (way > 0) == (part == 0):
                        ring.copy(part, way, step).start()
        for ring in rings:
            for way in (1, -1):
                ring.pick_step(way, step - 1)
    for ring in rings:
        ring.arrived(0, 1, 4)
        ring.arrived(1, -1, 4)
        ring.pick_step(1, 4)
    for stream in outward:
        stream.phase2(received=False)

    row, col = iota((CH, CH), 0), iota((CH, CH), 1)
    same = row // BLOCK == col // BLOCK
    ra, ca = row % BLOCK, col % BLOCK
    unpack = jnp.concatenate(
        [
            jnp.where(same & (ra < 6) & (ca == 6 + ra // 3) & (ra % 3 == j), 1.0, 0.0)
            for j in range(3)
        ],
        axis=1,
    ).astype(BF16)
    repack = [
        jnp.where(same & (ra >= 6) & (ca == 3 * (ra - 6) + j), 1.0, 0.0).astype(BF16)
        for j in range(3)
    ]
    real = (iota((CH, 1), 0) % BLOCK) < SLOTS
    spot = iota((CH, 128), 1) == iota((CH, 128), 0) % BLOCK
    wg, wu, wd = weights

    def rows_of(g):
        return pl.ds(pl.multiple_of(g * CH, CH), CH)

    def unpack_group(halves, ref, g):
        rows, zs = rows_of(g), pl.ds(2 * g, 2)
        chunks = []
        for j in range(3):
            lanes = slice(j * 128, (j + 1) * 128)
            low, high = (half[zs, :, :, :, lanes].reshape(CH, 128) for half in halves)
            ref[rows, lanes] = low
            ref[rows, 512 + j * 128 : 512 + (j + 1) * 128] = high
            chunks.append(jnp.concatenate([low, high], axis=1))
        last = dot(unpack, jnp.concatenate(chunks, axis=0)).astype(BF16)
        ref[rows, 384:512] = last[:, :128]
        ref[rows, 896:1024] = last[:, 128:]

    for one in loads:
        one.wait()
    for stream in outward[:2]:
        stream.arrived()

    def forward(g, _):
        rows = rows_of(g)
        unpack_group(gots[:2], x_s, g)
        x = x_s[rows, :]
        pre_gate = dot(x, wg[...])
        pre_up = dot(x, wu[...])
        sig = jax.nn.sigmoid(pre_gate)
        silu = jnp.where(real, pre_gate * sig, 0.0)
        h_s[rows, :] = (silu * pre_up).astype(BF16)
        silu_s[rows, :] = silu
        a_s[rows, :] = jnp.where(real, pre_up * sig * (1.0 + pre_gate * (1.0 - sig)), 0.0)
        return 0

    lax.fori_loop(0, 4, forward, 0)
    for stream in outward[2:]:
        stream.arrived()

    def backward(g, _):
        rows = rows_of(g)
        zs = pl.ds(2 * g, 2)
        unpack_group(gots[2:], s_s, g)
        hgrad = dot(s_s[rows, :], wd[...], ((1,), (1,)))
        d_gate = (hgrad * a_s[rows, :]).astype(BF16)
        d_up = (hgrad * silu_s[rows, :]).astype(BF16)
        dg_s[rows, :] = d_gate
        du_s[rows, :] = d_up
        product = jnp.sum(h_s[rows, :].astype(F32) * hgrad, axis=1, keepdims=True)
        spots = jnp.where(spot, product, 0.0).reshape(CH // BLOCK, BLOCK, 128)
        backs[2][zs] = jnp.sum(spots, axis=1).reshape(2, 8, 2, 1, 128)

        def route(cols):
            return dot(d_gate, wg[cols, :], ((1,), (1,))) + dot(d_up, wu[cols, :], ((1,), (1,)))

        tail = route(slice(3 * CH, 4 * CH)).astype(BF16)
        for j in range(3):
            part = route(slice(j * CH, (j + 1) * CH)) + dot(repack[j], tail)
            put_chunk(backs[:2], zs, j, part.astype(BF16))

        @pl.when(g > 0)
        def _():
            for stream in homeward:
                stream.group1(g - 1)

        return 0

    lax.fori_loop(0, 4, backward, 0)

    def grads(i, _):
        cols = pl.ds(pl.multiple_of(i * CH, CH), CH)
        x = x_s[:, cols]
        parts[0][i] = dot(x, dg_s[...], ((0,), (0,))).astype(BF16)
        parts[1][i] = dot(x, du_s[...], ((0,), (0,))).astype(BF16)
        parts[2][i] = dot(h_s[...], s_s[:, cols], ((0,), (0,))).astype(BF16)
        return 0

    lax.fori_loop(0, 4, grads, 0)
    for stream in homeward:
        stream.group1(3)

    def scatter_copy(k, i):
        target = (dp + i) % 4
        return pltpu.make_async_remote_copy(
            src_ref=parts[k].at[target],
            dst_ref=lands[k].at[dp],
            send_sem=send3.at[k, i],
            recv_sem=recv3.at[k],
            device_id=(target, me),
            device_id_type=pl.DeviceIdType.MESH,
        )

    for k in range(3):
        for i in (1, 3, 2):
            scatter_copy(k, i).start()
        pltpu.make_async_copy(parts[k].at[dp], lands[k].at[dp], recv3.at[k]).start()
    for stream in homeward:
        stream.phase2()
    for stream in homeward:
        stream.arrived()
    for ring in rings:
        for i in range(1, 8):
            for one in ring.small(i):
                one.wait_send()
        for step in range(1, 5):
            for part in range(2):
                for way in (1, -1):
                    if step < 4 or (way > 0) == (part == 0):
                        ring.copy(part, way, step).wait_send()
    for stream in outward:
        stream.sent2()
    for stream in homeward:
        stream.sent1()
        stream.sent2()
    for k in range(3):
        pltpu.make_async_copy(lands[k], lands[k], recv3.at[k]).wait()
        for i in (1, 3, 2):
            scatter_copy(k, i).wait_send()


def local(kernel, out_shape, args, scratch=(), name=None):
    return pl.pallas_call(
        kernel,
        out_shape=out_shape,
        in_specs=[VMEM] * len(args),
        out_specs=jax.tree.map(lambda _: VMEM, out_shape),
        scratch_shapes=scratch,
        compiler_params=pltpu.CompilerParams(vmem_limit_bytes=48 << 20),
        name=name,
    )(*args)


def shape(*dims, dtype=BF16):
    return jax.ShapeDtypeStruct(dims, dtype)


def shards(tokens, grad_out, expert_ids, gate_weight, w_gate, w_up, w_down):
    ids, gates = expert_ids.T, gate_weight.T
    half, small = (8, 8, 2, BLOCK, 384), (8, 8, 2, 1, 128)
    blocks = [(half, BF16), (half, BF16), (small, F32)]
    parts = [((4, 256, 384), BF16), ((4, 256, 384), BF16), ((4, 384, 256), BF16)]
    weights = [((1024, 384), BF16), ((1024, 384), BF16), ((384, 1024), BF16)]
    rows = [((ROWS, 1024), BF16)] * 2 + [((ROWS, 384), F32)] * 2 + [((ROWS, 384), BF16)] * 3
    ring = [((8, 2, 128, 512), BF16)] * 2 + [((8, 4, 128), jnp.int32)] * 2
    ring += [((8, 4, 128), BF16)] * 2 + [((4, 128), jnp.int32), ((4, 128), BF16)]
    sem = pltpu.SemaphoreType.DMA
    *home, land_gate, land_up, land_down = pl.pallas_call(
        main_kernel,
        out_shape=[shape(*dims, dtype=kind) for dims, kind in blocks + parts],
        in_specs=[pl.BlockSpec(memory_space=pl.ANY)] * 7,
        out_specs=[VMEM] * 6,
        scratch_shapes=[
            pltpu.VMEM(dims, kind)
            for dims, kind in ring + [(half, BF16)] * 8 + weights + rows + blocks * 2 + parts
        ]
        + [sem((3, 32)), sem((3,)), sem((7, 16)), sem((7,)), sem((3, 4)), sem((3,)), sem((3,))]
        + [sem((2, 4, 5)), sem((2, 4, 5)), sem((2, 2, 8)), sem((2, 2)), sem((6,))],
        compiler_params=pltpu.CompilerParams(
            collective_id=0, has_side_effects=True, vmem_limit_bytes=50 << 20
        ),
        name="main",
    )(ids, gates, tokens, grad_out, w_gate[0], w_up[0], w_down[0])
    home = [a.reshape(128, *a.shape[3:]) for a in home]
    sums = (land_gate, land_up, land_down)
    wide = shape(1, 256, 384, dtype=F32)
    grad_tokens, grad_gate, *grads = local(
        combine_kernel,
        (shape(128, 1024), shape(4, 128), wide, wide, shape(1, 384, 256, dtype=F32)),
        (ids, gates, *home, *sums),
        name="combine",
    )
    return (grad_tokens, grad_gate.T, *grads)


def solution(mesh):
    rows = P(("dp", "expert"), None)
    weights = P("expert", None, None)
    return jax.shard_map(
        shards,
        mesh=mesh,
        in_specs=(rows, rows, rows, rows, weights, weights, weights),
        out_specs=(rows, rows, P("expert", "dp", None), P("expert", "dp", None), P("expert", None, "dp")),
        check_vma=False,
    )
```

```python
import functools

import jax
import jax.numpy as jnp
from jax import lax
from jax.experimental import pallas as pl
from jax.experimental.pallas import tpu as pltpu
from jax.sharding import PartitionSpec as P

F32, BF16 = jnp.float32, jnp.bfloat16
SLOTS = 6
BLOCK = 8
ROWS = 1024
CH = 256
SPLIT = 1
VMEM = pl.BlockSpec(memory_space=pltpu.VMEM)


def dot(a, b, contract=((1,), (0,))):
    return lax.dot_general(a, b, (contract, ((), ())), preferred_element_type=F32)


def iota(shape, dim):
    return lax.broadcasted_iota(jnp.int32, shape, dim)


def one_hots(ids):
    experts = iota((128, 128), 0)
    named = jnp.zeros((128, 128), F32)
    for k in range(4):
        named = named + jnp.where(ids[k : k + 1, :] == experts, 1.0, 0.0)
    named = named.astype(BF16)
    earlier = jnp.where(iota((128, 128), 0) < iota((128, 128), 1), 1.0, 0.0).astype(BF16)
    rank = dot(named, earlier)
    rank = jnp.where(named.astype(F32) > 0.5, rank, -1.0)
    spread = jnp.where(iota((ROWS, 128), 0) // BLOCK == iota((ROWS, 128), 1), 1.0, 0.0).astype(BF16)
    ranks = dot(spread, rank.astype(BF16))
    place = (iota((ROWS, 128), 0) % BLOCK).astype(F32)
    main = jnp.where((ranks == place) & (place < 5.5), 1.0, 0.0)
    tails = [
        jnp.where((ranks == 3.0 * (place - 6.0) + j) & (place > 5.5), 1.0, 0.0) for j in range(3)
    ]
    return rank, main, tails, spread


def put_chunk(pieces, pair, j, rows):
    first, third, low, high = pieces
    for i, at in enumerate(pair):
        half = rows[i * 128 : (i + 1) * 128]
        if j == 1:
            low[at] = half[:, :128].reshape(8, 2, BLOCK, 128)
            high[at] = half[:, 128:].reshape(8, 2, BLOCK, 128)
        else:
            (third if j else first)[at] = half.reshape(8, 2, BLOCK, CH)


def get_chunk(pieces, j):
    first, third, low, high = pieces
    if j == 1:
        return jnp.concatenate(
            [low[...].reshape(ROWS, 128), high[...].reshape(ROWS, 128)], axis=1
        )
    return (third if j else first)[...].reshape(ROWS, CH)


def combine_kernel(
    ids_ref, gate_ref, *refs
):
    pieces, p_ref, sums = refs[:4], refs[4], refs[5:8]
    tok_ref, gate_out_ref, *grads = refs[8:13]
    copies = [pltpu.make_async_copy(sums[i], grads[i], refs[13].at[i]) for i in range(3)]
    for copy in copies:
        copy.start()
    ids = ids_ref[...]
    rank, main, tails, _ = one_hots(ids)
    main = main.astype(BF16)
    last = jnp.zeros((128, CH), F32)
    for j in range(3):
        part = get_chunk(pieces, j)
        tok_ref[:, j * CH : (j + 1) * CH] = dot(main, part, ((0,), (0,))).astype(BF16)
        last = last + dot(tails[j].astype(BF16), part, ((0,), (0,)))
    tok_ref[:, 3 * CH :] = last.astype(BF16)
    mine = jnp.zeros((128, 128), F32)
    for r in range(SLOTS):
        mine = mine + jnp.where(rank == r, p_ref[:, 0, r : r + 1], 0.0)
    gates = gate_ref[...].astype(F32)
    experts = iota((128, 128), 0)
    for k in range(4):
        total = jnp.sum(jnp.where(ids[k : k + 1, :] == experts, mine, 0.0), axis=0, keepdims=True)
        gate_out_ref[k : k + 1, :] = (total / gates[k : k + 1, :]).astype(BF16)
    for copy in copies:
        copy.wait()


def ring_step(i):
    return jnp.where(i % 2 == 1, (i + 1) // 2, 8 - i // 2)


class Exchange:
    def __init__(self, route, src, mid, dst, send1, recv1, send2, recv2):
        self.route, self.src, self.mid, self.dst = route, src, mid, dst
        self.send1, self.recv1, self.send2, self.recv2 = send1, recv1, send2, recv2
        self.dp, me = lax.axis_index("dp"), lax.axis_index("expert")
        self.z, self.y, self.c = me // 16, (me // 2) % 8, me % 2

    def slab(self, p):
        return self.src.at[p] if self.route == "z" else self.src.at[:, p]

    def landing(self):
        return self.dst.at[:, self.y, self.c] if self.route == "z" else self.dst.at[self.z, :, self.c]

    def peer(self, p, c):
        return p * 16 + self.y * 2 + c, self.z * 16 + p * 2 + c

    def along(self):
        return self.z if self.route == "z" else self.y

    def first(self, p):
        by_z, by_y = self.peer(p, self.c)
        return by_z if self.route == "z" else by_y

    def copy1(self, p):
        return pltpu.make_async_remote_copy(
            src_ref=self.slab(p),
            dst_ref=self.mid.at[self.along()],
            send_sem=self.send1.at[p],
            recv_sem=self.recv1,
            device_id=(self.dp, self.first(p)),
            device_id_type=pl.DeviceIdType.MESH,
        )

    def piece1(self, p, at):
        return pltpu.make_async_remote_copy(
            src_ref=self.src.at[at, p],
            dst_ref=self.mid.at[self.y, at],
            send_sem=self.send1.at[8 * at + p],
            recv_sem=self.recv1,
            device_id=(self.dp, self.first(p)),
            device_id_type=pl.DeviceIdType.MESH,
        )

    def group1(self, pair):
        for at in pair:
            if self.route == "z":

                @pl.when(at != self.z)
                def _():
                    self.copy1(at).start()

                @pl.when(at == self.z)
                def _():
                    pltpu.make_async_copy(self.slab(at), self.mid.at[at], self.recv1).start()

            else:

                def one(i, _):
                    self.piece1((self.y + ring_step(i)) % 8, at).start()
                    return 0

                lax.fori_loop(1, 8, one, 0)
                pltpu.make_async_copy(
                    self.src.at[at, self.y], self.mid.at[self.y, at], self.recv1
                ).start()

    def copy2(self, i):
        across = self.y if self.route == "z" else self.z
        p = (across + jnp.where(i < 14, ring_step(i // 2 + 1), 0)) % 8
        c = jnp.where(i < 14, i % 2, 1 - self.c)
        by_z, by_y = self.peer(p, c)
        return pltpu.make_async_remote_copy(
            src_ref=self.mid.at[:, p, c],
            dst_ref=self.landing(),
            send_sem=self.send2.at[i],
            recv_sem=self.recv2,
            device_id=(self.dp, by_y if self.route == "z" else by_z),
            device_id_type=pl.DeviceIdType.MESH,
        )

    def phase1(self):
        along = self.along()

        def one(i, _):
            self.copy1((along + ring_step(i)) % 8).start()
            return 0

        lax.fori_loop(1, 8, one, 0)
        pltpu.make_async_copy(self.slab(along), self.mid.at[along], self.recv1).start()

    def phase2(self, received=True):
        if received:
            pltpu.make_async_copy(self.mid, self.mid, self.recv1).wait()

        def one(i, _):
            self.copy2(i).start()
            return 0

        lax.fori_loop(0, 15, one, 0)
        across = self.y if self.route == "z" else self.z
        pltpu.make_async_copy(self.mid.at[:, across, self.c], self.landing(), self.recv2).start()

    def arrived(self):
        pltpu.make_async_copy(self.dst, self.dst, self.recv2).wait()

    def sent1(self, grouped):
        def one(i, _):
            p = (self.along() + i) % 8
            if grouped and self.route == "y":
                for at in range(8):
                    self.piece1(p, at).wait_send()
            else:
                self.copy1(p).wait_send()
            return 0

        lax.fori_loop(1, 8, one, 0)

    def sent2(self):
        def two(i, _):
            self.copy2(i).wait_send()
            return 0

        lax.fori_loop(0, 15, two, 0)


def greet():
    dp, me = lax.axis_index("dp"), lax.axis_index("expert")
    z, y, c = me // 16, (me // 2) % 8, me % 2
    barrier = pltpu.get_barrier_semaphore()

    def signal(target):
        pl.semaphore_signal(barrier, inc=1, device_id=target, device_id_type=pl.DeviceIdType.MESH)

    def rings(i, _):
        for core in (c, 1 - c):
            signal((dp, ((z + i) % 8) * 16 + y * 2 + core))
            signal((dp, z * 16 + ((y + i) % 8) * 2 + core))
        return 0

    lax.fori_loop(1, 8, rings, 0)
    signal((dp, z * 16 + y * 2 + 1 - c))
    for i in range(1, 4):
        signal(((dp + i) % 4, me))
    return barrier


class Ring:
    def __init__(self, number, inputs, ids, gates, held, held_ids, held_gates, xs, ss, send, recv, few, meta):
        self.number, self.inputs, self.ids, self.gates = number, inputs, ids, gates
        self.held, self.held_ids, self.held_gates = held, held_ids, held_gates
        self.xs, self.ss, self.send, self.recv, self.few, self.meta = xs, ss, send, recv, few, meta
        self.dp, me = lax.axis_index("dp"), lax.axis_index("expert")
        self.z, self.y, self.c = me // 16, (me // 2) % 8, me % 2
        self.at = self.y if number else self.z

    def device(self, p):
        if self.number:
            return (self.dp, self.z * 16 + p * 2 + self.c)
        return (self.dp, p * 16 + self.y * 2 + self.c)

    def own(self, part):
        return self.inputs[part].at[:, pl.ds(512 * self.number, 512)]

    def piece(self, block, q):
        count = 128 // SPLIT
        return self.held.at[block, q // SPLIT, pl.ds(q % SPLIT * count, count)]

    def own_piece(self, q):
        count = 128 // SPLIT
        rows = pl.ds(q % SPLIT * count, count)
        return self.inputs[q // SPLIT].at[rows, pl.ds(512 * self.number, 512)]

    def copy(self, q, way, step):
        block = (self.at - way * (step - 1) + 8) % 8
        which = q * 2 + (way > 0)
        return pltpu.make_async_remote_copy(
            src_ref=self.own_piece(q) if step == 1 else self.piece(block, q),
            dst_ref=self.piece(block, q),
            send_sem=self.send.at[which, step],
            recv_sem=self.recv.at[which, step],
            device_id=self.device((self.at + way + 8) % 8),
            device_id_type=pl.DeviceIdType.MESH,
        )

    def arrived(self, q, way, step):
        piece = self.piece((self.at - way * step + 8) % 8, q)
        pltpu.make_async_copy(piece, piece, self.recv.at[q * 2 + (way > 0), step]).wait()

    def small(self, i):
        for k, (src, dst) in enumerate(((self.ids, self.held_ids), (self.gates, self.held_gates))):
            yield pltpu.make_async_remote_copy(
                src_ref=src,
                dst_ref=dst.at[self.at],
                send_sem=self.few.at[k, i],
                recv_sem=self.meta.at[k],
                device_id=self.device((self.at + i) % 8),
                device_id_type=pl.DeviceIdType.MESH,
            )

    def pick(self, block, ids, gates):
        row = iota((128, 128), 0)
        place, receiver = (row % BLOCK).astype(F32), row // BLOCK
        if self.number:
            expert = receiver // 2 * 16 + self.y * 2 + receiver % 2
        else:
            expert = self.z * 16 + receiver
        named, gate = jnp.zeros((128, 128), F32), jnp.zeros((128, 128), F32)
        for k in range(4):
            hit = ids[k : k + 1, :] == expert
            named = jnp.where(hit, 1.0, named)
            gate = jnp.where(hit, gates[k : k + 1, :], gate)
        earlier = jnp.where(row < iota((128, 128), 1), 1.0, 0.0).astype(BF16)
        rank = jnp.where(named > 0.5, dot(named.astype(BF16), earlier), -1.0)
        main = jnp.where((rank == place) & (place < 5.5), 1.0, 0.0)
        held = self.held

        def chunk(j):
            return jnp.concatenate(
                [held[block, part, :, j * 128 : (j + 1) * 128] for part in range(2)], axis=1
            )

        last = chunk(3)
        for j in range(3):
            tail = jnp.where((rank == 3.0 * (place - 6.0) + j) & (place > 5.5), 1.0, 0.0)
            scale = jnp.sum((main + tail) * gate, axis=1, keepdims=True)
            choice = jnp.concatenate([main.astype(BF16), tail.astype(BF16)], axis=1)
            rows = dot(choice, jnp.concatenate([chunk(j), last], axis=0))
            lanes = slice(j * 128, (j + 1) * 128)
            self.xs[block, :, :, :, lanes] = rows[:, :128].astype(BF16).reshape(8, 2, 8, 128)
            self.ss[block, :, :, :, lanes] = (
                (rows[:, 128:] * scale).astype(BF16).reshape(8, 2, 8, 128)
            )

    def pick_step(self, way, step):
        block = (self.at - way * step + 8) % 8
        self.pick(block, self.held_ids[block], self.held_gates[block].astype(F32))


def main_kernel(*refs):
    refs = list(refs)
    take = lambda count: [refs.pop(0) for _ in range(count)]
    (ids, gates), inputs, weights_hbm = take(2), take(2), take(3)
    homes, sums, (my_ids, my_gates) = take(5), take(3), take(2)
    helds, held_ids, held_gates = take(2), take(2), take(2)
    mids, gots, weights = take(4), take(4), take(3)
    x_s, s_s, a_s, silu_s, dg_s, du_s, h_s = take(7)
    backs, back_mids, parts, lands = take(5), take(5), take(3), take(3)
    send1, recv1, send2, recv2, send3, recv3, load = take(7)
    ring_send, ring_recv, few, meta, mine = take(5)
    barrier = greet()
    dp, me = lax.axis_index("dp"), lax.axis_index("expert")
    rings = [
        Ring(
            t, inputs, ids, gates, helds[t], held_ids[t], held_gates[t], mids[t], mids[2 + t],
            ring_send.at[t], ring_recv.at[t], few.at[t], meta.at[t],
        )
        for t in range(2)
    ]
    outward = [
        Exchange("zyzy"[i], None, mids[i], gots[i], None, None, send2.at[i], recv2.at[i])
        for i in range(4)
    ]
    homeward = [
        Exchange(
            "zyzyz"[i], backs[i], back_mids[i], homes[i],
            send1.at[i], recv1.at[i], send2.at[4 + i], recv2.at[4 + i],
        )
        for i in range(5)
    ]
    locals_ = [
        pltpu.make_async_copy(ids, my_ids, mine.at[0]),
        pltpu.make_async_copy(gates, my_gates, mine.at[1]),
    ] + [
        pltpu.make_async_copy(ring.own(part), ring.held.at[ring.at, part], mine.at[2 + 2 * t + part])
        for t, ring in enumerate(rings)
        for part in range(2)
    ]
    loads = [pltpu.make_async_copy(weights_hbm[i], weights[i], load.at[i]) for i in range(3)]
    for one in locals_ + loads:
        one.start()
    for ring in rings:
        pltpu.make_async_copy(ids, ring.held_ids.at[ring.at], ring.meta.at[0]).start()
        pltpu.make_async_copy(gates, ring.held_gates.at[ring.at], ring.meta.at[1]).start()
    pl.semaphore_wait(barrier, 32)
    pieces = range(2 * SPLIT)
    for q in pieces:
        for ring in rings:
            for way in (1, -1):
                ring.copy(q, way, 1).start()
    for i in range(1, 8):
        for ring in rings:
            for one in ring.small(i):
                one.start()
    for one in locals_:
        one.wait()
    for ring in rings:
        ring.pick(ring.at, my_ids[...], my_gates[...].astype(F32))
    for step in range(2, 5):
        for q in pieces:
            for ring in rings:
                for way in (1, -1):
                    ring.arrived(q, way, step - 1)
                    if step < 4 or (way > 0) == (q < SPLIT):
                        ring.copy(q, way, step).start()
        for ring in rings:
            if step == 2:
                pltpu.make_async_copy(ring.held_ids, ring.held_ids, ring.meta.at[0]).wait()
                pltpu.make_async_copy(ring.held_gates, ring.held_gates, ring.meta.at[1]).wait()
            for way in (1, -1):
                ring.pick_step(way, step - 1)
    for ring in rings:
        for q in pieces:
            ring.arrived(q, 1 if q < SPLIT else -1, 4)
        ring.pick_step(1, 4)
    for stream in outward:
        stream.phase2(received=False)

    row, col = iota((CH, CH), 0), iota((CH, CH), 1)
    same = row // BLOCK == col // BLOCK
    ra, ca = row % BLOCK, col % BLOCK
    unpack = jnp.concatenate(
        [
            jnp.where(same & (ra < 6) & (ca == 6 + ra // 3) & (ra % 3 == j), 1.0, 0.0)
            for j in range(3)
        ],
        axis=1,
    ).astype(BF16)
    repack = [
        jnp.where(same & (ra >= 6) & (ca == 3 * (ra - 6) + j), 1.0, 0.0).astype(BF16)
        for j in range(3)
    ]
    real = (iota((CH, 1), 0) % BLOCK) < SLOTS
    spot = iota((CH, 128), 1) == iota((CH, 128), 0) % BLOCK
    wg, wu, wd = weights

    def rows_of(g):
        return pl.ds(pl.multiple_of(g * CH, CH), CH)

    z = me // 16

    def pair_of(g):
        far = jnp.where(g < 3, 3 - g, 4)
        return (z + far) % 8, (z + jnp.where(g < 3, 8 - far, 0)) % 8

    def unpack_group(halves, ref, g):
        rows, pair = rows_of(g), pair_of(g)
        chunks = []
        for j in range(3):
            lanes = slice(j * 128, (j + 1) * 128)
            low, high = (
                jnp.concatenate([half[at, :, :, :, lanes].reshape(128, 128) for at in pair], axis=0)
                for half in halves
            )
            ref[rows, lanes] = low
            ref[rows, 512 + j * 128 : 512 + (j + 1) * 128] = high
            chunks.append(jnp.concatenate([low, high], axis=1))
        last = dot(unpack, jnp.concatenate(chunks, axis=0)).astype(BF16)
        ref[rows, 384:512] = last[:, :128]
        ref[rows, 896:1024] = last[:, 128:]

    for one in loads:
        one.wait()
    for stream in outward[:2]:
        stream.arrived()

    def forward(g, _):
        rows = rows_of(g)
        unpack_group(gots[:2], x_s, g)
        x = x_s[rows, :]
        pre_gate = dot(x, wg[...])
        pre_up = dot(x, wu[...])
        sig = jax.nn.sigmoid(pre_gate)
        silu = jnp.where(real, pre_gate * sig, 0.0)
        h_s[rows, :] = (silu * pre_up).astype(BF16)
        silu_s[rows, :] = silu
        a_s[rows, :] = jnp.where(real, pre_up * sig * (1.0 + pre_gate * (1.0 - sig)), 0.0)
        return 0

    lax.fori_loop(0, 4, forward, 0)
    for stream in outward[2:]:
        stream.arrived()

    def backward(g, _):
        rows, pair = rows_of(g), pair_of(g)
        unpack_group(gots[2:], s_s, g)
        hgrad = dot(s_s[rows, :], wd[...], ((1,), (1,)))
        d_gate = (hgrad * a_s[rows, :]).astype(BF16)
        d_up = (hgrad * silu_s[rows, :]).astype(BF16)
        dg_s[rows, :] = d_gate
        du_s[rows, :] = d_up
        product = jnp.sum(h_s[rows, :].astype(F32) * hgrad, axis=1, keepdims=True)
        spots = jnp.where(spot, product, 0.0).reshape(CH // BLOCK, BLOCK, 128)
        spots = jnp.sum(spots, axis=1)
        for i, at in enumerate(pair):
            backs[4][at] = spots[i * 16 : (i + 1) * 16].reshape(8, 2, 1, 128)

        def route(cols):
            return dot(d_gate, wg[cols, :], ((1,), (1,))) + dot(d_up, wu[cols, :], ((1,), (1,)))

        tail = route(slice(3 * CH, 4 * CH)).astype(BF16)
        for j in range(3):
            part = route(slice(j * CH, (j + 1) * CH)) + dot(repack[j], tail)
            put_chunk(backs[:4], pair, j, part.astype(BF16))

        @pl.when(g > 0)
        def _():
            for stream in homeward[:2]:
                stream.group1(pair_of(g - 1))

        return 0

    lax.fori_loop(0, 4, backward, 0)

    def grads(i, _):
        cols = pl.ds(pl.multiple_of(i * CH, CH), CH)
        x = x_s[:, cols]
        parts[0][i] = dot(x, dg_s[...], ((0,), (0,))).astype(BF16)
        parts[1][i] = dot(x, du_s[...], ((0,), (0,))).astype(BF16)
        parts[2][i] = dot(h_s[...], s_s[:, cols], ((0,), (0,))).astype(BF16)
        return 0

    lax.fori_loop(0, 4, grads, 0)
    for stream in homeward[:2]:
        stream.group1(pair_of(3))
    for stream in homeward[2:]:
        stream.phase1()

    def scatter_copy(k, i):
        target = (dp + i) % 4
        return pltpu.make_async_remote_copy(
            src_ref=parts[k].at[target],
            dst_ref=lands[k].at[dp],
            send_sem=send3.at[k, i],
            recv_sem=recv3.at[k],
            device_id=(target, me),
            device_id_type=pl.DeviceIdType.MESH,
        )

    for k in range(3):
        for i in (1, 3, 2):
            scatter_copy(k, i).start()
        pltpu.make_async_copy(parts[k].at[dp], lands[k].at[dp], recv3.at[k]).start()
    for stream in homeward:
        stream.phase2()
    for k in range(3):
        pltpu.make_async_copy(lands[k], lands[k], recv3.at[k]).wait()
        sums[k][0] = sum(lands[k][i].astype(F32) for i in range(1, 4)) + lands[k][0].astype(F32)
    for stream in homeward:
        stream.arrived()
    for ring in rings:
        for i in range(1, 8):
            for one in ring.small(i):
                one.wait_send()
        for step in range(1, 5):
            for q in pieces:
                for way in (1, -1):
                    if step < 4 or (way > 0) == (q < SPLIT):
                        ring.copy(q, way, step).wait_send()
    for stream in outward:
        stream.sent2()
    for i, stream in enumerate(homeward):
        stream.sent1(grouped=i < 2)
        stream.sent2()
    for k in range(3):
        for i in (1, 3, 2):
            scatter_copy(k, i).wait_send()


def shape(*dims, dtype=BF16):
    return jax.ShapeDtypeStruct(dims, dtype)


def shards(tokens, grad_out, expert_ids, gate_weight, w_gate, w_up, w_down):
    ids, gates = expert_ids.T, gate_weight.T
    inputs = (ids, gates, tokens, grad_out, w_gate[0], w_up[0], w_down[0])
    half, small = (8, 8, 2, BLOCK, 384), (8, 8, 2, 1, 128)
    lanes = [(8, 8, 2, BLOCK, n) for n in (256, 256, 128, 128)]
    blocks = [(dims, BF16) for dims in lanes] + [(small, F32)]
    parts = [((4, 256, 384), BF16), ((4, 256, 384), BF16), ((4, 384, 256), BF16)]
    totals = [((1, 256, 384), F32), ((1, 256, 384), F32), ((1, 384, 256), F32)]
    weights = [((1024, 384), BF16), ((1024, 384), BF16), ((384, 1024), BF16)]
    rows = [((ROWS, 1024), BF16)] * 2 + [((ROWS, 384), F32)] * 2 + [((ROWS, 384), BF16)] * 3
    ring = [((8, 2, 128, 512), BF16)] * 2 + [((8, 4, 128), jnp.int32)] * 2
    ring += [((8, 4, 128), BF16)] * 2
    routes = [((4, 128), jnp.int32), ((4, 128), BF16)]
    sem = pltpu.SemaphoreType.DMA
    *home, sum_gate, sum_up, sum_down, my_ids, my_gates = pl.pallas_call(
        main_kernel,
        out_shape=[shape(*dims, dtype=kind) for dims, kind in blocks + totals + routes],
        in_specs=[pl.BlockSpec(memory_space=pltpu.HBM)] * 7,
        out_specs=[VMEM] * 10,
        scratch_shapes=[
            pltpu.VMEM(dims, kind)
            for dims, kind in ring + [(half, BF16)] * 8 + weights + rows + blocks * 2 + parts * 2
        ]
        + [sem((5, 64)), sem((5,)), sem((9, 16)), sem((9,)), sem((3, 4)), sem((3,)), sem((3,))]
        + [sem((2, 4 * SPLIT, 5)), sem((2, 4 * SPLIT, 5)), sem((2, 2, 8)), sem((2, 2)), sem((6,))],
        compiler_params=pltpu.CompilerParams(
            collective_id=0, has_side_effects=True, vmem_limit_bytes=50 << 20
        ),
        name="main",
    )(*[pltpu.with_memory_space_constraint(a, pltpu.HBM) for a in inputs])
    home = [a.reshape(128, *a.shape[3:]) for a in home]
    sums = (sum_gate, sum_up, sum_down)
    args = (my_ids, my_gates, *home, *sums)
    hbm = pl.BlockSpec(memory_space=pltpu.HBM)
    grad_tokens, grad_gate, *grads = pl.pallas_call(
        combine_kernel,
        out_shape=[shape(128, 1024), shape(4, 128)] + [shape(*d, dtype=kind) for d, kind in totals],
        in_specs=[VMEM] * len(args),
        out_specs=[VMEM, VMEM, hbm, hbm, hbm],
        scratch_shapes=[sem((3,))],
        compiler_params=pltpu.CompilerParams(vmem_limit_bytes=24 << 20),
        name="combine",
    )(*args)
    return (grad_tokens, grad_gate.T, *grads)


def solution(mesh):
    rows = P(("dp", "expert"), None)
    weights = P("expert", None, None)
    return jax.shard_map(
        shards,
        mesh=mesh,
        in_specs=(rows, rows, rows, rows, weights, weights, weights),
        out_specs=(rows, rows, P("expert", "dp", None), P("expert", "dp", None), P("expert", None, "dp")),
        check_vma=False,
    )
```

```python
import functools

import jax
import jax.numpy as jnp
from jax import lax
from jax.experimental import pallas as pl
from jax.experimental.pallas import tpu as pltpu
from jax.sharding import PartitionSpec as P

F32, BF16 = jnp.float32, jnp.bfloat16
SLOTS = 6
BLOCK = 8
ROWS = 1024
CH = 256
SPLIT = 2
VMEM = pl.BlockSpec(memory_space=pltpu.VMEM)


def dot(a, b, contract=((1,), (0,))):
    return lax.dot_general(a, b, (contract, ((), ())), preferred_element_type=F32)


def iota(shape, dim):
    return lax.broadcasted_iota(jnp.int32, shape, dim)


def one_hots(ids):
    experts = iota((128, 128), 0)
    named = jnp.zeros((128, 128), F32)
    for k in range(4):
        named = named + jnp.where(ids[k : k + 1, :] == experts, 1.0, 0.0)
    named = named.astype(BF16)
    earlier = jnp.where(iota((128, 128), 0) < iota((128, 128), 1), 1.0, 0.0).astype(BF16)
    rank = dot(named, earlier)
    rank = jnp.where(named.astype(F32) > 0.5, rank, -1.0)
    spread = jnp.where(iota((ROWS, 128), 0) // BLOCK == iota((ROWS, 128), 1), 1.0, 0.0).astype(BF16)
    ranks = dot(spread, rank.astype(BF16))
    place = (iota((ROWS, 128), 0) % BLOCK).astype(F32)
    main = jnp.where((ranks == place) & (place < 5.5), 1.0, 0.0)
    tails = [
        jnp.where((ranks == 3.0 * (place - 6.0) + j) & (place > 5.5), 1.0, 0.0) for j in range(3)
    ]
    return rank, main.astype(BF16), [tail.astype(BF16) for tail in tails]


def put_chunk(pieces, pair, j, rows):
    first, third, low, high = pieces
    for i, at in enumerate(pair):
        half = rows[i * 128 : (i + 1) * 128]
        if j == 1:
            low[at] = half[:, :128].reshape(8, 2, BLOCK, 128)
            high[at] = half[:, 128:].reshape(8, 2, BLOCK, 128)
        else:
            (third if j else first)[at] = half.reshape(8, 2, BLOCK, CH)


def combine_kernel(*refs):
    ids, gates = refs[0][...], refs[1][...].astype(F32)
    low, high, p_ref, early, last, rank, main, tail = refs[2:10]
    sums, (tok_ref, gate_out_ref), grads, sem = refs[10:13], refs[13:15], refs[15:18], refs[18]
    copies = [pltpu.make_async_copy(sums[i], grads[i], sem.at[i]) for i in range(3)]
    for copy in copies:
        copy.start()
    part = jnp.concatenate([low[...].reshape(ROWS, 128), high[...].reshape(ROWS, 128)], axis=1)
    tok_ref[:, :CH] = early[:, :CH]
    tok_ref[:, CH : 2 * CH] = dot(main[...], part, ((0,), (0,))).astype(BF16)
    tok_ref[:, 2 * CH : 3 * CH] = early[:, CH:]
    tok_ref[:, 3 * CH :] = (last[...] + dot(tail[...], part, ((0,), (0,)))).astype(BF16)
    mine = jnp.zeros((128, 128), F32)
    for r in range(SLOTS):
        mine = mine + jnp.where(rank[...] == r, p_ref[:, 0, r : r + 1], 0.0)
    experts = iota((128, 128), 0)
    for k in range(4):
        total = jnp.sum(jnp.where(ids[k : k + 1, :] == experts, mine, 0.0), axis=0, keepdims=True)
        gate_out_ref[k : k + 1, :] = (total / gates[k : k + 1, :]).astype(BF16)
    for copy in copies:
        copy.wait()


def ring_step(i):
    return jnp.where(i % 2 == 1, 4 - i // 2, 4 + i // 2)


class Exchange:
    def __init__(self, route, src, mid, dst, send1, recv1, send2, recv2):
        self.route, self.src, self.mid, self.dst = route, src, mid, dst
        self.send1, self.recv1, self.send2, self.recv2 = send1, recv1, send2, recv2
        self.dp, me = lax.axis_index("dp"), lax.axis_index("expert")
        self.z, self.y, self.c = me // 16, (me // 2) % 8, me % 2

    def slab(self, p):
        return self.src.at[p] if self.route == "z" else self.src.at[:, p]

    def landing(self):
        return self.dst.at[:, self.y, self.c] if self.route == "z" else self.dst.at[self.z, :, self.c]

    def peer(self, p, c):
        return p * 16 + self.y * 2 + c, self.z * 16 + p * 2 + c

    def along(self):
        return self.z if self.route == "z" else self.y

    def first(self, p):
        by_z, by_y = self.peer(p, self.c)
        return by_z if self.route == "z" else by_y

    def copy1(self, p):
        return pltpu.make_async_remote_copy(
            src_ref=self.slab(p),
            dst_ref=self.mid.at[self.along()],
            send_sem=self.send1.at[p],
            recv_sem=self.recv1,
            device_id=(self.dp, self.first(p)),
            device_id_type=pl.DeviceIdType.MESH,
        )

    def piece1(self, p, at):
        return pltpu.make_async_remote_copy(
            src_ref=self.src.at[at, p],
            dst_ref=self.mid.at[self.y, at],
            send_sem=self.send1.at[8 * at + p],
            recv_sem=self.recv1,
            device_id=(self.dp, self.first(p)),
            device_id_type=pl.DeviceIdType.MESH,
        )

    def group1(self, pair):
        for at in pair:
            if self.route == "z":

                @pl.when(at != self.z)
                def _():
                    self.copy1(at).start()

                @pl.when(at == self.z)
                def _():
                    pltpu.make_async_copy(self.slab(at), self.mid.at[at], self.recv1).start()

            else:

                def one(i, _):
                    self.piece1((self.y + ring_step(i)) % 8, at).start()
                    return 0

                lax.fori_loop(1, 8, one, 0)
                pltpu.make_async_copy(
                    self.src.at[at, self.y], self.mid.at[self.y, at], self.recv1
                ).start()

    def copy2(self, i):
        across = self.y if self.route == "z" else self.z
        p = (across + jnp.where(i < 14, ring_step(i // 2 + 1), 0)) % 8
        c = jnp.where(i < 14, i % 2, 1 - self.c)
        by_z, by_y = self.peer(p, c)
        return pltpu.make_async_remote_copy(
            src_ref=self.mid.at[:, p, c],
            dst_ref=self.landing(),
            send_sem=self.send2.at[i],
            recv_sem=self.recv2,
            device_id=(self.dp, by_y if self.route == "z" else by_z),
            device_id_type=pl.DeviceIdType.MESH,
        )

    def phase1(self):
        along = self.along()

        def one(i, _):
            self.copy1((along + ring_step(i)) % 8).start()
            return 0

        lax.fori_loop(1, 8, one, 0)
        pltpu.make_async_copy(self.slab(along), self.mid.at[along], self.recv1).start()

    def phase2(self, received=True):
        if received:
            pltpu.make_async_copy(self.mid, self.mid, self.recv1).wait()

        def one(i, _):
            self.copy2(i).start()
            return 0

        lax.fori_loop(0, 15, one, 0)
        across = self.y if self.route == "z" else self.z
        pltpu.make_async_copy(self.mid.at[:, across, self.c], self.landing(), self.recv2).start()

    def arrived(self):
        pltpu.make_async_copy(self.dst, self.dst, self.recv2).wait()

    def sent1(self, grouped):
        def one(i, _):
            p = (self.along() + i) % 8
            if grouped and self.route == "y":
                for at in range(8):
                    self.piece1(p, at).wait_send()
            else:
                self.copy1(p).wait_send()
            return 0

        lax.fori_loop(1, 8, one, 0)

    def sent2(self):
        def two(i, _):
            self.copy2(i).wait_send()
            return 0

        lax.fori_loop(0, 15, two, 0)


def greet():
    dp, me = lax.axis_index("dp"), lax.axis_index("expert")
    z, y, c = me // 16, (me // 2) % 8, me % 2
    barrier = pltpu.get_barrier_semaphore()

    def signal(target):
        pl.semaphore_signal(barrier, inc=1, device_id=target, device_id_type=pl.DeviceIdType.MESH)

    def rings(i, _):
        for core in (c, 1 - c):
            signal((dp, ((z + i) % 8) * 16 + y * 2 + core))
            signal((dp, z * 16 + ((y + i) % 8) * 2 + core))
        return 0

    lax.fori_loop(1, 8, rings, 0)
    signal((dp, z * 16 + y * 2 + 1 - c))
    for i in range(1, 4):
        signal(((dp + i) % 4, me))
    return barrier


class Ring:
    def __init__(self, number, inputs, ids, gates, held, held_ids, held_gates, xs, ss, send, recv, few, meta):
        self.number, self.inputs, self.ids, self.gates = number, inputs, ids, gates
        self.held, self.held_ids, self.held_gates = held, held_ids, held_gates
        self.xs, self.ss, self.send, self.recv, self.few, self.meta = xs, ss, send, recv, few, meta
        self.dp, me = lax.axis_index("dp"), lax.axis_index("expert")
        self.z, self.y, self.c = me // 16, (me // 2) % 8, me % 2
        self.at = self.y if number else self.z

    def device(self, p):
        if self.number:
            return (self.dp, self.z * 16 + p * 2 + self.c)
        return (self.dp, p * 16 + self.y * 2 + self.c)

    def own(self, part):
        return self.inputs[part].at[:, pl.ds(512 * self.number, 512)]

    def piece(self, block, q):
        count = 128 // SPLIT
        return self.held.at[block, q // SPLIT, pl.ds(q % SPLIT * count, count)]

    def own_piece(self, q):
        count = 128 // SPLIT
        rows = pl.ds(q % SPLIT * count, count)
        return self.inputs[q // SPLIT].at[rows, pl.ds(512 * self.number, 512)]

    def copy(self, q, way, step):
        block = (self.at - way * (step - 1) + 8) % 8
        which = q * 2 + (way > 0)
        return pltpu.make_async_remote_copy(
            src_ref=self.own_piece(q) if step == 1 else self.piece(block, q),
            dst_ref=self.piece(block, q),
            send_sem=self.send.at[which, step],
            recv_sem=self.recv.at[which, step],
            device_id=self.device((self.at + way + 8) % 8),
            device_id_type=pl.DeviceIdType.MESH,
        )

    def arrived(self, q, way, step):
        piece = self.piece((self.at - way * step + 8) % 8, q)
        pltpu.make_async_copy(piece, piece, self.recv.at[q * 2 + (way > 0), step]).wait()

    def small(self, i):
        for k, (src, dst) in enumerate(((self.ids, self.held_ids), (self.gates, self.held_gates))):
            yield pltpu.make_async_remote_copy(
                src_ref=src,
                dst_ref=dst.at[self.at],
                send_sem=self.few.at[k, i],
                recv_sem=self.meta.at[k],
                device_id=self.device((self.at + i) % 8),
                device_id_type=pl.DeviceIdType.MESH,
            )

    def pick(self, block, ids, gates, parts=(0, 1)):
        row = iota((128, 128), 0)
        place, receiver = (row % BLOCK).astype(F32), row // BLOCK
        if self.number:
            expert = receiver // 2 * 16 + self.y * 2 + receiver % 2
        else:
            expert = self.z * 16 + receiver
        named, gate = jnp.zeros((128, 128), F32), jnp.zeros((128, 128), F32)
        for k in range(4):
            hit = ids[k : k + 1, :] == expert
            named = jnp.where(hit, 1.0, named)
            gate = jnp.where(hit, gates[k : k + 1, :], gate)
        earlier = jnp.where(row < iota((128, 128), 1), 1.0, 0.0).astype(BF16)
        rank = jnp.where(named > 0.5, dot(named.astype(BF16), earlier), -1.0)
        main = jnp.where((rank == place) & (place < 5.5), 1.0, 0.0)
        held = self.held

        def chunk(j):
            return jnp.concatenate(
                [held[block, part, :, j * 128 : (j + 1) * 128] for part in parts], axis=1
            )

        last = chunk(3)
        for j in range(3):
            tail = jnp.where((rank == 3.0 * (place - 6.0) + j) & (place > 5.5), 1.0, 0.0)
            choice = jnp.concatenate([main.astype(BF16), tail.astype(BF16)], axis=1)
            rows = dot(choice, jnp.concatenate([chunk(j), last], axis=0))
            lanes = slice(j * 128, (j + 1) * 128)
            if 0 in parts:
                self.xs[block, :, :, :, lanes] = rows[:, :128].astype(BF16).reshape(8, 2, 8, 128)
            if 1 in parts:
                scale = jnp.sum((main + tail) * gate, axis=1, keepdims=True)
                self.ss[block, :, :, :, lanes] = (
                    (rows[:, -128:] * scale).astype(BF16).reshape(8, 2, 8, 128)
                )

    def pick_step(self, way, step, parts=(0, 1)):
        block = (self.at - way * step + 8) % 8
        self.pick(block, self.held_ids[block], self.held_gates[block].astype(F32), parts)


def main_kernel(*refs):
    refs = list(refs)
    take = lambda count: [refs.pop(0) for _ in range(count)]
    (ids, gates), inputs, weights_hbm = take(2), take(2), take(3)
    late, sums, (my_ids, my_gates) = take(3), take(3), take(2)
    early, last_s, rank_s, main_s, tail_s = take(5)
    homes = take(2) + late
    helds, held_ids, held_gates = take(2), take(2), take(2)
    mids, gots, weights = take(4), take(4), take(3)
    x_s, s_s, a_s, silu_s, dg_s, du_s, h_s = take(7)
    backs, back_mids, parts, lands = take(5), take(5), take(3), take(3)
    send1, recv1, send2, recv2, send3, recv3, load = take(7)
    ring_send, ring_recv, few, meta, mine = take(5)
    barrier = greet()
    dp, me = lax.axis_index("dp"), lax.axis_index("expert")
    rings = [
        Ring(
            t, inputs, ids, gates, helds[t], held_ids[t], held_gates[t], mids[t], mids[2 + t],
            ring_send.at[t], ring_recv.at[t], few.at[t], meta.at[t],
        )
        for t in range(2)
    ]
    outward = [
        Exchange("zyzy"[i], None, mids[i], gots[i], None, None, send2.at[i], recv2.at[i])
        for i in range(4)
    ]
    homeward = [
        Exchange(
            "zyzyz"[i], backs[i], back_mids[i], homes[i],
            send1.at[i], recv1.at[i], send2.at[4 + i], recv2.at[4 + i],
        )
        for i in range(5)
    ]
    locals_ = [
        pltpu.make_async_copy(ids, my_ids, mine.at[0]),
        pltpu.make_async_copy(gates, my_gates, mine.at[1]),
    ] + [
        pltpu.make_async_copy(ring.own(part), ring.held.at[ring.at, part], mine.at[2 + 2 * t + part])
        for t, ring in enumerate(rings)
        for part in range(2)
    ]
    loads = [pltpu.make_async_copy(weights_hbm[i], weights[i], load.at[i]) for i in range(3)]
    for one in locals_ + loads:
        one.start()
    for ring in rings:
        pltpu.make_async_copy(ids, ring.held_ids.at[ring.at], ring.meta.at[0]).start()
        pltpu.make_async_copy(gates, ring.held_gates.at[ring.at], ring.meta.at[1]).start()
    pl.semaphore_wait(barrier, 32)
    pieces = range(2 * SPLIT)
    for q in pieces:
        for ring in rings:
            for way in (1, -1):
                ring.copy(q, way, 1).start()
    for i in range(1, 8):
        for ring in rings:
            for one in ring.small(i):
                one.start()
    for one in locals_:
        one.wait()
    for ring in rings:
        ring.pick(ring.at, my_ids[...], my_gates[...].astype(F32))
    for step in range(2, 5):
        for q in pieces:
            for ring in rings:
                for way in (1, -1):
                    ring.arrived(q, way, step - 1)
                    if step < 4 or (way > 0) == (q % 2 == 0):
                        ring.copy(q, way, step).start()
        for ring in rings:
            if step == 2:
                pltpu.make_async_copy(ring.held_ids, ring.held_ids, ring.meta.at[0]).wait()
                pltpu.make_async_copy(ring.held_gates, ring.held_gates, ring.meta.at[1]).wait()
            for way in (1, -1):
                ring.pick_step(way, step - 1)
    for ring in rings:
        for q in pieces[:SPLIT]:
            ring.arrived(q, 1 if q % 2 == 0 else -1, 4)
        ring.pick_step(1, 4, (0,))
    for stream in outward[:2]:
        stream.phase2(received=False)
    for ring in rings:
        for q in pieces[SPLIT:]:
            ring.arrived(q, 1 if q % 2 == 0 else -1, 4)
        ring.pick_step(1, 4, (1,))
    for stream in outward[2:]:
        stream.phase2(received=False)

    row, col = iota((CH, CH), 0), iota((CH, CH), 1)
    same = row // BLOCK == col // BLOCK
    ra, ca = row % BLOCK, col % BLOCK
    unpack = jnp.concatenate(
        [
            jnp.where(same & (ra < 6) & (ca == 6 + ra // 3) & (ra % 3 == j), 1.0, 0.0)
            for j in range(3)
        ],
        axis=1,
    ).astype(BF16)
    repack = [
        jnp.where(same & (ra >= 6) & (ca == 3 * (ra - 6) + j), 1.0, 0.0).astype(BF16)
        for j in range(3)
    ]
    real = (iota((CH, 1), 0) % BLOCK) < SLOTS
    spot = iota((CH, 128), 1) == iota((CH, 128), 0) % BLOCK
    wg, wu, wd = weights

    def rows_of(g):
        return pl.ds(pl.multiple_of(g * CH, CH), CH)

    z = me // 16

    def pair_of(g):
        far = 4 - g
        return (z + far) % 8, (z + jnp.where(g > 0, 8 - far, 0)) % 8

    def unpack_group(halves, ref, g):
        rows, pair = rows_of(g), pair_of(g)
        chunks = []
        for j in range(3):
            lanes = slice(j * 128, (j + 1) * 128)
            low, high = (
                jnp.concatenate([half[at, :, :, :, lanes].reshape(128, 128) for at in pair], axis=0)
                for half in halves
            )
            ref[rows, lanes] = low
            ref[rows, 512 + j * 128 : 512 + (j + 1) * 128] = high
            chunks.append(jnp.concatenate([low, high], axis=1))
        last = dot(unpack, jnp.concatenate(chunks, axis=0)).astype(BF16)
        ref[rows, 384:512] = last[:, :128]
        ref[rows, 896:1024] = last[:, 128:]

    for one in loads:
        one.wait()
    for stream in outward[:2]:
        stream.arrived()

    def forward(g, _):
        rows = rows_of(g)
        unpack_group(gots[:2], x_s, g)
        x = x_s[rows, :]
        pre_gate = dot(x, wg[...])
        pre_up = dot(x, wu[...])
        sig = jax.nn.sigmoid(pre_gate)
        silu = jnp.where(real, pre_gate * sig, 0.0)
        h_s[rows, :] = (silu * pre_up).astype(BF16)
        silu_s[rows, :] = silu
        a_s[rows, :] = jnp.where(real, pre_up * sig * (1.0 + pre_gate * (1.0 - sig)), 0.0)
        return 0

    lax.fori_loop(0, 4, forward, 0)
    for stream in outward[2:]:
        stream.arrived()

    def backward(g, _):
        rows, pair = rows_of(g), pair_of(g)
        unpack_group(gots[2:], s_s, g)
        hgrad = dot(s_s[rows, :], wd[...], ((1,), (1,)))
        d_gate = (hgrad * a_s[rows, :]).astype(BF16)
        d_up = (hgrad * silu_s[rows, :]).astype(BF16)
        dg_s[rows, :] = d_gate
        du_s[rows, :] = d_up
        product = jnp.sum(h_s[rows, :].astype(F32) * hgrad, axis=1, keepdims=True)
        spots = jnp.where(spot, product, 0.0).reshape(CH // BLOCK, BLOCK, 128)
        spots = jnp.sum(spots, axis=1)
        for i, at in enumerate(pair):
            backs[4][at] = spots[i * 16 : (i + 1) * 16].reshape(8, 2, 1, 128)

        def route(cols):
            return dot(d_gate, wg[cols, :], ((1,), (1,))) + dot(d_up, wu[cols, :], ((1,), (1,)))

        tail = route(slice(3 * CH, 4 * CH)).astype(BF16)
        for j in range(3):
            part = route(slice(j * CH, (j + 1) * CH)) + dot(repack[j], tail)
            put_chunk(backs[:4], pair, j, part.astype(BF16))

        @pl.when(g > 0)
        def _():
            for stream in homeward[:2]:
                stream.group1(pair_of(g - 1))

        return 0

    lax.fori_loop(0, 4, backward, 0)

    def grads(i, _):
        cols = pl.ds(pl.multiple_of(i * CH, CH), CH)
        x = x_s[:, cols]
        parts[0][i] = dot(x, dg_s[...], ((0,), (0,))).astype(BF16)
        parts[1][i] = dot(x, du_s[...], ((0,), (0,))).astype(BF16)
        parts[2][i] = dot(h_s[...], s_s[:, cols], ((0,), (0,))).astype(BF16)
        return 0

    lax.fori_loop(0, 4, grads, 0)
    for stream in homeward[:2]:
        stream.group1(pair_of(3))
    for stream in homeward[2:]:
        stream.phase1()

    def scatter_copy(k, i):
        target = (dp + i) % 4
        return pltpu.make_async_remote_copy(
            src_ref=parts[k].at[target],
            dst_ref=lands[k].at[dp],
            send_sem=send3.at[k, i],
            recv_sem=recv3.at[k],
            device_id=(target, me),
            device_id_type=pl.DeviceIdType.MESH,
        )

    for k in range(3):
        for i in (1, 3, 2):
            scatter_copy(k, i).start()
        pltpu.make_async_copy(parts[k].at[dp], lands[k].at[dp], recv3.at[k]).start()
    for stream in homeward:
        stream.phase2()
    for k in range(3):
        pltpu.make_async_copy(lands[k], lands[k], recv3.at[k]).wait()
        sums[k][0] = sum(lands[k][i].astype(F32) for i in range(1, 4)) + lands[k][0].astype(F32)
    rank, main, tails = one_hots(my_ids[...])
    rank_s[...] = rank
    main_s[...] = main
    tail_s[...] = tails[1]
    for stream in homeward[:2]:
        stream.arrived()
    first, third = homes[0][...].reshape(ROWS, CH), homes[1][...].reshape(ROWS, CH)
    early[:, :CH] = dot(main, first, ((0,), (0,))).astype(BF16)
    early[:, CH:] = dot(main, third, ((0,), (0,))).astype(BF16)
    last_s[...] = dot(tails[0], first, ((0,), (0,))) + dot(tails[2], third, ((0,), (0,)))
    for stream in homeward[2:]:
        stream.arrived()
    for ring in rings:
        for i in range(1, 8):
            for one in ring.small(i):
                one.wait_send()
        for step in range(1, 5):
            for q in pieces:
                for way in (1, -1):
                    if step < 4 or (way > 0) == (q % 2 == 0):
                        ring.copy(q, way, step).wait_send()
    for stream in outward:
        stream.sent2()
    for i, stream in enumerate(homeward):
        stream.sent1(grouped=i < 2)
        stream.sent2()
    for k in range(3):
        for i in (1, 3, 2):
            scatter_copy(k, i).wait_send()


def shape(*dims, dtype=BF16):
    return jax.ShapeDtypeStruct(dims, dtype)


def shards(tokens, grad_out, expert_ids, gate_weight, w_gate, w_up, w_down):
    ids, gates = expert_ids.T, gate_weight.T
    inputs = (ids, gates, tokens, grad_out, w_gate[0], w_up[0], w_down[0])
    half, small = (8, 8, 2, BLOCK, 384), (8, 8, 2, 1, 128)
    lanes = [(8, 8, 2, BLOCK, n) for n in (256, 256, 128, 128)]
    blocks = [(dims, BF16) for dims in lanes] + [(small, F32)]
    parts = [((4, 256, 384), BF16), ((4, 256, 384), BF16), ((4, 384, 256), BF16)]
    totals = [((1, 256, 384), F32), ((1, 256, 384), F32), ((1, 384, 256), F32)]
    weights = [((1024, 384), BF16), ((1024, 384), BF16), ((384, 1024), BF16)]
    rows = [((ROWS, 1024), BF16)] * 2 + [((ROWS, 384), F32)] * 2 + [((ROWS, 384), BF16)] * 3
    ring = [((8, 2, 128, 512), BF16)] * 2 + [((8, 4, 128), jnp.int32)] * 2
    ring += [((8, 4, 128), BF16)] * 2
    routes = [((4, 128), jnp.int32), ((4, 128), BF16)]
    combine = [((128, 2 * CH), BF16), ((128, CH), F32), ((128, 128), F32)]
    combine += [((ROWS, 128), BF16)] * 2
    sem = pltpu.SemaphoreType.DMA
    outs = pl.pallas_call(
        main_kernel,
        out_shape=[shape(*dims, dtype=kind) for dims, kind in blocks[2:] + totals + routes + combine],
        in_specs=[pl.BlockSpec(memory_space=pltpu.HBM)] * 7,
        out_specs=[VMEM] * 13,
        scratch_shapes=[
            pltpu.VMEM(dims, kind)
            for dims, kind in blocks[:2] + ring + [(half, BF16)] * 8 + weights + rows + blocks * 2 + parts * 2
        ]
        + [sem((5, 64)), sem((5,)), sem((9, 16)), sem((9,)), sem((3, 4)), sem((3,)), sem((3,))]
        + [sem((2, 4 * SPLIT, 5)), sem((2, 4 * SPLIT, 5)), sem((2, 2, 8)), sem((2, 2)), sem((6,))],
        compiler_params=pltpu.CompilerParams(
            collective_id=0, has_side_effects=True, vmem_limit_bytes=50 << 20
        ),
        name="main",
    )(*[pltpu.with_memory_space_constraint(a, pltpu.HBM) for a in inputs])
    late = [a.reshape(128, *a.shape[3:]) for a in outs[:3]]
    args = (*outs[6:8], *late, *outs[8:], *outs[3:6])
    hbm = pl.BlockSpec(memory_space=pltpu.HBM)
    grad_tokens, grad_gate, *grads = pl.pallas_call(
        combine_kernel,
        out_shape=[shape(128, 1024), shape(4, 128)] + [shape(*d, dtype=kind) for d, kind in totals],
        in_specs=[VMEM] * len(args),
        out_specs=[VMEM, VMEM, hbm, hbm, hbm],
        scratch_shapes=[sem((3,))],
        compiler_params=pltpu.CompilerParams(vmem_limit_bytes=24 << 20),
        name="combine",
    )(*args)
    return (grad_tokens, grad_gate.T, *grads)


def solution(mesh):
    rows = P(("dp", "expert"), None)
    weights = P("expert", None, None)
    return jax.shard_map(
        shards,
        mesh=mesh,
        in_specs=(rows, rows, rows, rows, weights, weights, weights),
        out_specs=(rows, rows, P("expert", "dp", None), P("expert", "dp", None), P("expert", None, "dp")),
        check_vma=False,
    )
```

```python
import functools

import jax
import jax.numpy as jnp
from jax import lax
from jax.experimental import pallas as pl
from jax.experimental.pallas import tpu as pltpu
from jax.sharding import PartitionSpec as P

F32, BF16 = jnp.float32, jnp.bfloat16
SLOTS = 6
BLOCK = 8
ROWS = 1024
CH = 256
SPLIT = 2
VMEM = pl.BlockSpec(memory_space=pltpu.VMEM)


def dot(a, b, contract=((1,), (0,))):
    return lax.dot_general(a, b, (contract, ((), ())), preferred_element_type=F32)


def iota(shape, dim):
    return lax.broadcasted_iota(jnp.int32, shape, dim)


def one_hots(ids):
    experts = iota((128, 128), 0)
    named = jnp.zeros((128, 128), F32)
    for k in range(4):
        named = named + jnp.where(ids[k : k + 1, :] == experts, 1.0, 0.0)
    named = named.astype(BF16)
    earlier = jnp.where(iota((128, 128), 0) < iota((128, 128), 1), 1.0, 0.0).astype(BF16)
    rank = dot(named, earlier)
    rank = jnp.where(named.astype(F32) > 0.5, rank, -1.0)
    spread = jnp.where(iota((ROWS, 128), 0) // BLOCK == iota((ROWS, 128), 1), 1.0, 0.0).astype(BF16)
    ranks = dot(spread, rank.astype(BF16))
    place = (iota((ROWS, 128), 0) % BLOCK).astype(F32)
    main = jnp.where((ranks == place) & (place < 5.5), 1.0, 0.0)
    tails = [
        jnp.where((ranks == 3.0 * (place - 6.0) + j) & (place > 5.5), 1.0, 0.0) for j in range(3)
    ]
    return rank, main.astype(BF16), [tail.astype(BF16) for tail in tails]


def put_chunk(pieces, pair, j, rows):
    first, third, low, high = pieces
    for i, at in enumerate(pair):
        half = rows[i * 128 : (i + 1) * 128]
        if j == 1:
            low[at] = half[:, :128].reshape(8, 2, BLOCK, 128)
            high[at] = half[:, 128:].reshape(8, 2, BLOCK, 128)
        else:
            (third if j else first)[at] = half.reshape(8, 2, BLOCK, CH)


def combine_kernel(*refs):
    ids, gates = refs[0][...], refs[1][...].astype(F32)
    low, high, p_ref, early, last, rank, main, tail = refs[2:10]
    sums, (tok_ref, gate_out_ref), grads, sem = refs[10:13], refs[13:15], refs[15:18], refs[18]
    copies = [pltpu.make_async_copy(sums[i], grads[i], sem.at[i]) for i in range(3)]
    for copy in copies:
        copy.start()
    part = jnp.concatenate([low[...].reshape(ROWS, 128), high[...].reshape(ROWS, 128)], axis=1)
    tok_ref[:, :CH] = early[:, :CH]
    tok_ref[:, CH : 2 * CH] = dot(main[...], part, ((0,), (0,))).astype(BF16)
    tok_ref[:, 2 * CH : 3 * CH] = early[:, CH:]
    tok_ref[:, 3 * CH :] = (last[...] + dot(tail[...], part, ((0,), (0,)))).astype(BF16)
    mine = jnp.zeros((128, 128), F32)
    for r in range(SLOTS):
        mine = mine + jnp.where(rank[...] == r, p_ref[:, 0, r : r + 1], 0.0)
    experts = iota((128, 128), 0)
    for k in range(4):
        total = jnp.sum(jnp.where(ids[k : k + 1, :] == experts, mine, 0.0), axis=0, keepdims=True)
        gate_out_ref[k : k + 1, :] = (total / gates[k : k + 1, :]).astype(BF16)
    for copy in copies:
        copy.wait()


def ring_step(i):
    return jnp.where(i % 2 == 1, 4 - i // 2, 4 + i // 2)


class Exchange:
    def __init__(self, route, src, mid, dst, send1, recv1, send2, recv2):
        self.route, self.src, self.mid, self.dst = route, src, mid, dst
        self.send1, self.recv1, self.send2, self.recv2 = send1, recv1, send2, recv2
        self.dp, me = lax.axis_index("dp"), lax.axis_index("expert")
        self.z, self.y, self.c = me // 16, (me // 2) % 8, me % 2

    def slab(self, p):
        return self.src.at[p] if self.route == "z" else self.src.at[:, p]

    def landing(self):
        return self.dst.at[:, self.y, self.c] if self.route == "z" else self.dst.at[self.z, :, self.c]

    def peer(self, p, c):
        return p * 16 + self.y * 2 + c, self.z * 16 + p * 2 + c

    def along(self):
        return self.z if self.route == "z" else self.y

    def first(self, p):
        by_z, by_y = self.peer(p, self.c)
        return by_z if self.route == "z" else by_y

    def copy1(self, p):
        return pltpu.make_async_remote_copy(
            src_ref=self.slab(p),
            dst_ref=self.mid.at[self.along()],
            send_sem=self.send1.at[p],
            recv_sem=self.recv1,
            device_id=(self.dp, self.first(p)),
            device_id_type=pl.DeviceIdType.MESH,
        )

    def piece1(self, p, at):
        return pltpu.make_async_remote_copy(
            src_ref=self.src.at[at, p],
            dst_ref=self.mid.at[self.y, at],
            send_sem=self.send1.at[8 * at + p],
            recv_sem=self.recv1,
            device_id=(self.dp, self.first(p)),
            device_id_type=pl.DeviceIdType.MESH,
        )

    def group1(self, pair):
        for at in pair:
            if self.route == "z":

                @pl.when(at != self.z)
                def _():
                    self.copy1(at).start()

                @pl.when(at == self.z)
                def _():
                    pltpu.make_async_copy(self.slab(at), self.mid.at[at], self.recv1).start()

            else:

                def one(i, _):
                    self.piece1((self.y + ring_step(i)) % 8, at).start()
                    return 0

                lax.fori_loop(1, 8, one, 0)
                pltpu.make_async_copy(
                    self.src.at[at, self.y], self.mid.at[self.y, at], self.recv1
                ).start()

    def copy2(self, i):
        across = self.y if self.route == "z" else self.z
        p = (across + jnp.where(i < 14, ring_step(i // 2 + 1), 0)) % 8
        c = jnp.where(i < 14, i % 2, 1 - self.c)
        by_z, by_y = self.peer(p, c)
        return pltpu.make_async_remote_copy(
            src_ref=self.mid.at[:, p, c],
            dst_ref=self.landing(),
            send_sem=self.send2.at[i],
            recv_sem=self.recv2,
            device_id=(self.dp, by_y if self.route == "z" else by_z),
            device_id_type=pl.DeviceIdType.MESH,
        )

    def phase1(self):
        along = self.along()

        def one(i, _):
            self.copy1((along + ring_step(i)) % 8).start()
            return 0

        lax.fori_loop(1, 8, one, 0)
        pltpu.make_async_copy(self.slab(along), self.mid.at[along], self.recv1).start()

    def phase2(self, received=True):
        if received:
            pltpu.make_async_copy(self.mid, self.mid, self.recv1).wait()

        def one(i, _):
            self.copy2(i).start()
            return 0

        lax.fori_loop(0, 15, one, 0)
        across = self.y if self.route == "z" else self.z
        pltpu.make_async_copy(self.mid.at[:, across, self.c], self.landing(), self.recv2).start()

    def arrived(self):
        pltpu.make_async_copy(self.dst, self.dst, self.recv2).wait()

    def sent1(self, grouped):
        def one(i, _):
            p = (self.along() + i) % 8
            if grouped and self.route == "y":
                for at in range(8):
                    self.piece1(p, at).wait_send()
            else:
                self.copy1(p).wait_send()
            return 0

        lax.fori_loop(1, 8, one, 0)

    def sent2(self):
        def two(i, _):
            self.copy2(i).wait_send()
            return 0

        lax.fori_loop(0, 15, two, 0)


def greet():
    dp, me = lax.axis_index("dp"), lax.axis_index("expert")
    z, y, c = me // 16, (me // 2) % 8, me % 2
    barrier = pltpu.get_barrier_semaphore()

    def signal(target):
        pl.semaphore_signal(barrier, inc=1, device_id=target, device_id_type=pl.DeviceIdType.MESH)

    def rings(i, _):
        for core in (c, 1 - c):
            signal((dp, ((z + i) % 8) * 16 + y * 2 + core))
            signal((dp, z * 16 + ((y + i) % 8) * 2 + core))
        return 0

    lax.fori_loop(1, 8, rings, 0)
    signal((dp, z * 16 + y * 2 + 1 - c))
    for i in range(1, 4):
        signal(((dp + i) % 4, me))
    return barrier


class Ring:
    def __init__(self, number, inputs, ids, gates, held, held_ids, held_gates, xs, ss, send, recv, few, meta):
        self.number, self.inputs, self.ids, self.gates = number, inputs, ids, gates
        self.held, self.held_ids, self.held_gates = held, held_ids, held_gates
        self.xs, self.ss, self.send, self.recv, self.few, self.meta = xs, ss, send, recv, few, meta
        self.dp, me = lax.axis_index("dp"), lax.axis_index("expert")
        self.z, self.y, self.c = me // 16, (me // 2) % 8, me % 2
        self.at = self.y if number else self.z

    def device(self, p):
        if self.number:
            return (self.dp, self.z * 16 + p * 2 + self.c)
        return (self.dp, p * 16 + self.y * 2 + self.c)

    def own(self, part):
        return self.inputs[part].at[:, pl.ds(512 * self.number, 512)]

    def piece(self, block, q):
        count = 128 // SPLIT
        return self.held.at[block, q // SPLIT, pl.ds(q % SPLIT * count, count)]

    def own_piece(self, q):
        count = 128 // SPLIT
        rows = pl.ds(q % SPLIT * count, count)
        return self.inputs[q // SPLIT].at[rows, pl.ds(512 * self.number, 512)]

    def copy(self, q, way, step):
        block = (self.at - way * (step - 1) + 8) % 8
        which = q * 2 + (way > 0)
        return pltpu.make_async_remote_copy(
            src_ref=self.own_piece(q) if step == 1 else self.piece(block, q),
            dst_ref=self.piece(block, q),
            send_sem=self.send.at[which, step],
            recv_sem=self.recv.at[which, step],
            device_id=self.device((self.at + way + 8) % 8),
            device_id_type=pl.DeviceIdType.MESH,
        )

    def arrived(self, q, way, step):
        piece = self.piece((self.at - way * step + 8) % 8, q)
        pltpu.make_async_copy(piece, piece, self.recv.at[q * 2 + (way > 0), step]).wait()

    def small(self, i):
        for k, (src, dst) in enumerate(((self.ids, self.held_ids), (self.gates, self.held_gates))):
            yield pltpu.make_async_remote_copy(
                src_ref=src,
                dst_ref=dst.at[self.at],
                send_sem=self.few.at[k, i],
                recv_sem=self.meta.at[k],
                device_id=self.device((self.at + i) % 8),
                device_id_type=pl.DeviceIdType.MESH,
            )

    def pick(self, block, ids, gates, parts=(0, 1)):
        row = iota((128, 128), 0)
        place, receiver = (row % BLOCK).astype(F32), row // BLOCK
        if self.number:
            expert = receiver // 2 * 16 + self.y * 2 + receiver % 2
        else:
            expert = self.z * 16 + receiver
        named, gate = jnp.zeros((128, 128), F32), jnp.zeros((128, 128), F32)
        for k in range(4):
            hit = ids[k : k + 1, :] == expert
            named = jnp.where(hit, 1.0, named)
            gate = jnp.where(hit, gates[k : k + 1, :], gate)
        earlier = jnp.where(row < iota((128, 128), 1), 1.0, 0.0).astype(BF16)
        rank = jnp.where(named > 0.5, dot(named.astype(BF16), earlier), -1.0)
        main = jnp.where((rank == place) & (place < 5.5), 1.0, 0.0)
        held = self.held

        def chunk(j):
            return jnp.concatenate(
                [held[block, part, :, j * 128 : (j + 1) * 128] for part in parts], axis=1
            )

        last = chunk(3)
        for j in range(3):
            tail = jnp.where((rank == 3.0 * (place - 6.0) + j) & (place > 5.5), 1.0, 0.0)
            choice = jnp.concatenate([main.astype(BF16), tail.astype(BF16)], axis=1)
            rows = dot(choice, jnp.concatenate([chunk(j), last], axis=0))
            lanes = slice(j * 128, (j + 1) * 128)
            if 0 in parts:
                self.xs[block, :, :, :, lanes] = rows[:, :128].astype(BF16).reshape(8, 2, 8, 128)
            if 1 in parts:
                scale = jnp.sum((main + tail) * gate, axis=1, keepdims=True)
                self.ss[block, :, :, :, lanes] = (
                    (rows[:, -128:] * scale).astype(BF16).reshape(8, 2, 8, 128)
                )

    def pick_step(self, way, step, parts=(0, 1)):
        block = (self.at - way * step + 8) % 8
        self.pick(block, self.held_ids[block], self.held_gates[block].astype(F32), parts)


def main_kernel(*refs):
    refs = list(refs)
    take = lambda count: [refs.pop(0) for _ in range(count)]
    (ids, gates), inputs, weights_hbm = take(2), take(2), take(3)
    late, sums, (my_ids, my_gates) = take(3), take(3), take(2)
    early, last_s, rank_s, main_s, tail_s = take(5)
    homes = take(2) + late
    helds, held_ids, held_gates = take(2), take(2), take(2)
    mids, gots, weights = take(4), take(4), take(3)
    x_s, s_s, a_s, silu_s, dg_s, du_s, h_s = take(7)
    backs, back_mids, parts, lands = take(5), take(5), take(3), take(3)
    send1, recv1, send2, recv2, send3, recv3, load = take(7)
    ring_send, ring_recv, few, meta, mine = take(5)
    barrier = greet()
    dp, me = lax.axis_index("dp"), lax.axis_index("expert")
    rings = [
        Ring(
            t, inputs, ids, gates, helds[t], held_ids[t], held_gates[t], mids[t], mids[2 + t],
            ring_send.at[t], ring_recv.at[t], few.at[t], meta.at[t],
        )
        for t in range(2)
    ]
    outward = [
        Exchange("zyzy"[i], None, mids[i], gots[i], None, None, send2.at[i], recv2.at[i])
        for i in range(4)
    ]
    homeward = [
        Exchange(
            "zyzyz"[i], backs[i], back_mids[i], homes[i],
            send1.at[i], recv1.at[i], send2.at[4 + i], recv2.at[4 + i],
        )
        for i in range(5)
    ]
    locals_ = [
        pltpu.make_async_copy(ids, my_ids, mine.at[0]),
        pltpu.make_async_copy(gates, my_gates, mine.at[1]),
    ] + [
        pltpu.make_async_copy(ring.own(part), ring.held.at[ring.at, part], mine.at[2 + 2 * t + part])
        for t, ring in enumerate(rings)
        for part in range(2)
    ]
    loads = [pltpu.make_async_copy(weights_hbm[i], weights[i], load.at[i]) for i in range(3)]
    for one in locals_ + loads:
        one.start()
    for ring in rings:
        pltpu.make_async_copy(ids, ring.held_ids.at[ring.at], ring.meta.at[0]).start()
        pltpu.make_async_copy(gates, ring.held_gates.at[ring.at], ring.meta.at[1]).start()
    pl.semaphore_wait(barrier, 32)
    pieces = range(2 * SPLIT)
    for q in pieces:
        for ring in rings:
            for way in (1, -1):
                ring.copy(q, way, 1).start()
    for i in range(1, 8):
        for ring in rings:
            for one in ring.small(i):
                one.start()
    for one in locals_:
        one.wait()
    for ring in rings:
        ring.pick(ring.at, my_ids[...], my_gates[...].astype(F32))
    for step in range(2, 5):
        for q in pieces:
            for ring in rings:
                for way in (1, -1):
                    ring.arrived(q, way, step - 1)
                    if step < 4 or (way > 0) == (q % 2 == 0):
                        ring.copy(q, way, step).start()
        for ring in rings:
            if step == 2:
                pltpu.make_async_copy(ring.held_ids, ring.held_ids, ring.meta.at[0]).wait()
                pltpu.make_async_copy(ring.held_gates, ring.held_gates, ring.meta.at[1]).wait()
            for way in (1, -1):
                ring.pick_step(way, step - 1)
    for ring in rings:
        for q in pieces[:SPLIT]:
            ring.arrived(q, 1 if q % 2 == 0 else -1, 4)
        ring.pick_step(1, 4, (0,))
    for stream in outward[:2]:
        stream.phase2(received=False)
    for ring in rings:
        for q in pieces[SPLIT:]:
            ring.arrived(q, 1 if q % 2 == 0 else -1, 4)
        ring.pick_step(1, 4, (1,))
    for stream in outward[2:]:
        stream.phase2(received=False)

    row, col = iota((CH, CH), 0), iota((CH, CH), 1)
    same = row // BLOCK == col // BLOCK
    ra, ca = row % BLOCK, col % BLOCK
    unpack = jnp.concatenate(
        [
            jnp.where(same & (ra < 6) & (ca == 6 + ra // 3) & (ra % 3 == j), 1.0, 0.0)
            for j in range(3)
        ],
        axis=1,
    ).astype(BF16)
    repack = [
        jnp.where(same & (ra >= 6) & (ca == 3 * (ra - 6) + j), 1.0, 0.0).astype(BF16)
        for j in range(3)
    ]
    real = (iota((CH, 1), 0) % BLOCK) < SLOTS
    spot = iota((CH, 128), 1) == iota((CH, 128), 0) % BLOCK
    wg, wu, wd = weights

    def rows_of(g):
        return pl.ds(pl.multiple_of(g * CH, CH), CH)

    z = me // 16

    def pair_of(g):
        far = 4 - g
        return (z + far) % 8, (z + jnp.where(g > 0, 8 - far, 0)) % 8

    def unpack_group(halves, ref, g):
        rows, pair = rows_of(g), pair_of(g)
        chunks = []
        for j in range(3):
            lanes = slice(j * 128, (j + 1) * 128)
            low, high = (
                jnp.concatenate([half[at, :, :, :, lanes].reshape(128, 128) for at in pair], axis=0)
                for half in halves
            )
            ref[rows, lanes] = low
            ref[rows, 512 + j * 128 : 512 + (j + 1) * 128] = high
            chunks.append(jnp.concatenate([low, high], axis=1))
        last = dot(unpack, jnp.concatenate(chunks, axis=0)).astype(BF16)
        ref[rows, 384:512] = last[:, :128]
        ref[rows, 896:1024] = last[:, 128:]

    for one in loads:
        one.wait()
    for stream in outward[:2]:
        stream.arrived()

    def forward(g, _):
        rows = rows_of(g)
        unpack_group(gots[:2], x_s, g)
        x = x_s[rows, :]
        pre_gate = dot(x, wg[...])
        pre_up = dot(x, wu[...])
        sig = jax.nn.sigmoid(pre_gate)
        silu = jnp.where(real, pre_gate * sig, 0.0)
        h_s[rows, :] = (silu * pre_up).astype(BF16)
        silu_s[rows, :] = silu
        a_s[rows, :] = jnp.where(real, pre_up * sig * (1.0 + pre_gate * (1.0 - sig)), 0.0)
        return 0

    lax.fori_loop(0, 4, forward, 0)
    for stream in outward[2:]:
        stream.arrived()

    def backward(g, _):
        rows, pair = rows_of(g), pair_of(g)
        unpack_group(gots[2:], s_s, g)
        hgrad = dot(s_s[rows, :], wd[...], ((1,), (1,)))
        d_gate = (hgrad * a_s[rows, :]).astype(BF16)
        d_up = (hgrad * silu_s[rows, :]).astype(BF16)
        @pl.when(g > 0)
        def _():
            for stream in homeward[:2]:
                stream.group1(pair_of(g - 1))

        dg_s[rows, :] = d_gate
        du_s[rows, :] = d_up
        product = jnp.sum(h_s[rows, :].astype(F32) * hgrad, axis=1, keepdims=True)
        spots = jnp.where(spot, product, 0.0).reshape(CH // BLOCK, BLOCK, 128)
        spots = jnp.sum(spots, axis=1)
        for i, at in enumerate(pair):
            backs[4][at] = spots[i * 16 : (i + 1) * 16].reshape(8, 2, 1, 128)

        def route(cols):
            return dot(d_gate, wg[cols, :], ((1,), (1,))) + dot(d_up, wu[cols, :], ((1,), (1,)))

        tail = route(slice(3 * CH, 4 * CH)).astype(BF16)
        for j in range(3):
            part = route(slice(j * CH, (j + 1) * CH)) + dot(repack[j], tail)
            put_chunk(backs[:4], pair, j, part.astype(BF16))

        return 0

    lax.fori_loop(0, 4, backward, 0)

    def grads(i, _):
        cols = pl.ds(pl.multiple_of(i * CH, CH), CH)
        x = x_s[:, cols]
        parts[0][i] = dot(x, dg_s[...], ((0,), (0,))).astype(BF16)
        parts[1][i] = dot(x, du_s[...], ((0,), (0,))).astype(BF16)
        parts[2][i] = dot(h_s[...], s_s[:, cols], ((0,), (0,))).astype(BF16)
        return 0

    lax.fori_loop(0, 1, grads, 0)
    for stream in homeward[:2]:
        stream.group1(pair_of(3))
    for stream in homeward[2:]:
        stream.phase1()
    lax.fori_loop(1, 4, grads, 0)

    def scatter_copy(k, i):
        target = (dp + i) % 4
        return pltpu.make_async_remote_copy(
            src_ref=parts[k].at[target],
            dst_ref=lands[k].at[dp],
            send_sem=send3.at[k, i],
            recv_sem=recv3.at[k],
            device_id=(target, me),
            device_id_type=pl.DeviceIdType.MESH,
        )

    for k in range(3):
        for i in (1, 3, 2):
            scatter_copy(k, i).start()
        pltpu.make_async_copy(parts[k].at[dp], lands[k].at[dp], recv3.at[k]).start()
    for stream in homeward:
        stream.phase2()
    for k in range(3):
        pltpu.make_async_copy(lands[k], lands[k], recv3.at[k]).wait()
        sums[k][0] = sum(lands[k][i].astype(F32) for i in range(1, 4)) + lands[k][0].astype(F32)
    rank, main, tails = one_hots(my_ids[...])
    rank_s[...] = rank
    main_s[...] = main
    tail_s[...] = tails[1]
    for stream in homeward[:2]:
        stream.arrived()
    first, third = homes[0][...].reshape(ROWS, CH), homes[1][...].reshape(ROWS, CH)
    early[:, :CH] = dot(main, first, ((0,), (0,))).astype(BF16)
    early[:, CH:] = dot(main, third, ((0,), (0,))).astype(BF16)
    last_s[...] = dot(tails[0], first, ((0,), (0,))) + dot(tails[2], third, ((0,), (0,)))
    for stream in homeward[2:]:
        stream.arrived()
    for ring in rings:
        for i in range(1, 8):
            for one in ring.small(i):
                one.wait_send()
        for step in range(1, 5):
            for q in pieces:
                for way in (1, -1):
                    if step < 4 or (way > 0) == (q % 2 == 0):
                        ring.copy(q, way, step).wait_send()
    for stream in outward:
        stream.sent2()
    for i, stream in enumerate(homeward):
        stream.sent1(grouped=i < 2)
        stream.sent2()
    for k in range(3):
        for i in (1, 3, 2):
            scatter_copy(k, i).wait_send()


def shape(*dims, dtype=BF16):
    return jax.ShapeDtypeStruct(dims, dtype)


def shards(tokens, grad_out, expert_ids, gate_weight, w_gate, w_up, w_down):
    ids, gates = expert_ids.T, gate_weight.T
    inputs = (ids, gates, tokens, grad_out, w_gate[0], w_up[0], w_down[0])
    half, small = (8, 8, 2, BLOCK, 384), (8, 8, 2, 1, 128)
    lanes = [(8, 8, 2, BLOCK, n) for n in (256, 256, 128, 128)]
    blocks = [(dims, BF16) for dims in lanes] + [(small, F32)]
    parts = [((4, 256, 384), BF16), ((4, 256, 384), BF16), ((4, 384, 256), BF16)]
    totals = [((1, 256, 384), F32), ((1, 256, 384), F32), ((1, 384, 256), F32)]
    weights = [((1024, 384), BF16), ((1024, 384), BF16), ((384, 1024), BF16)]
    rows = [((ROWS, 1024), BF16)] * 2 + [((ROWS, 384), F32)] * 2 + [((ROWS, 384), BF16)] * 3
    ring = [((8, 2, 128, 512), BF16)] * 2 + [((8, 4, 128), jnp.int32)] * 2
    ring += [((8, 4, 128), BF16)] * 2
    routes = [((4, 128), jnp.int32), ((4, 128), BF16)]
    combine = [((128, 2 * CH), BF16), ((128, CH), F32), ((128, 128), F32)]
    combine += [((ROWS, 128), BF16)] * 2
    sem = pltpu.SemaphoreType.DMA
    outs = pl.pallas_call(
        main_kernel,
        out_shape=[shape(*dims, dtype=kind) for dims, kind in blocks[2:] + totals + routes + combine],
        in_specs=[pl.BlockSpec(memory_space=pltpu.HBM)] * 7,
        out_specs=[VMEM] * 13,
        scratch_shapes=[
            pltpu.VMEM(dims, kind)
            for dims, kind in blocks[:2] + ring + [(half, BF16)] * 8 + weights + rows + blocks * 2 + parts * 2
        ]
        + [sem((5, 64)), sem((5,)), sem((9, 16)), sem((9,)), sem((3, 4)), sem((3,)), sem((3,))]
        + [sem((2, 4 * SPLIT, 5)), sem((2, 4 * SPLIT, 5)), sem((2, 2, 8)), sem((2, 2)), sem((6,))],
        compiler_params=pltpu.CompilerParams(
            collective_id=0, has_side_effects=True, vmem_limit_bytes=50 << 20
        ),
        name="main",
    )(*[pltpu.with_memory_space_constraint(a, pltpu.HBM) for a in inputs])
    late = [a.reshape(128, *a.shape[3:]) for a in outs[:3]]
    args = (*outs[6:8], *late, *outs[8:], *outs[3:6])
    hbm = pl.BlockSpec(memory_space=pltpu.HBM)
    grad_tokens, grad_gate, *grads = pl.pallas_call(
        combine_kernel,
        out_shape=[shape(128, 1024), shape(4, 128)] + [shape(*d, dtype=kind) for d, kind in totals],
        in_specs=[VMEM] * len(args),
        out_specs=[VMEM, VMEM, hbm, hbm, hbm],
        scratch_shapes=[sem((3,))],
        compiler_params=pltpu.CompilerParams(vmem_limit_bytes=24 << 20),
        name="combine",
    )(*args)
    return (grad_tokens, grad_gate.T, *grads)


def solution(mesh):
    rows = P(("dp", "expert"), None)
    weights = P("expert", None, None)
    return jax.shard_map(
        shards,
        mesh=mesh,
        in_specs=(rows, rows, rows, rows, weights, weights, weights),
        out_specs=(rows, rows, P("expert", "dp", None), P("expert", "dp", None), P("expert", None, "dp")),
        check_vma=False,
    )
```
